256 devices in a mesh: ctx: 128 (over z, x_lo, y, core), head: 2 (over x_hi).
Axes of the slice: x: 4 (x_hi: 2, x_lo: 2; x = x_hi * 2 + x_lo), y: 4, z: 8, core: 2. Of those that a mesh axis runs over, the one named last changes fastest.
Arguments:
- queries: bfloat16 [65536, 2048], P('ctx', 'head'), may hold values from -13 to 13, as said below
- keys: bfloat16 [65536, 512], P('ctx', 'head'), may hold values from -13 to 13
- values: bfloat16 [65536, 512], P('ctx', 'head'), may hold values from -24 to 24
- positions: int32 [65536], P('ctx'), may hold values from 0 to 32767, as said below
- out_weight: bfloat16 [2048, 4096], P(None, 'head'), may hold values from -0.125 to 0.125
Outputs:
- mixed: bfloat16 [65536, 4096], P('ctx', 'head')
The draws below stay inside these ranges and needn't reach their ends.
Inputs may be any that keep to these rules, and one draw needn't show every extreme that they name: queries, keys: every entry lies in the stated range. positions[r] is 0 where the token at sequence position g(r) begins a document and one more than the position of the token at g(r) - 1 otherwise; documents begin at sequence positions 0 and 32768 and possibly elsewhere in the first half; the second half is one document.
All inputs are finite; a program needn't handle non-finite values.
Results may differ from the reference program's by a relative error of at most 0.012.
The reference program's roundings to bfloat16 on the way count: a program that leaves them out, or rounds other values in their place, can miss the bound.
Values may be sent and summed in bfloat16 or wider, within the bound.
A program may use at most 128 MiB of HBM per device.

```python
import math
import jax
import jax.numpy as jnp
import numpy as np
from jax import lax

D = 4096
QUERY_HEADS = 16
KEY_VALUE_HEADS = 4
HEAD_SIZE = 128
STEPS = 4
BLOCK_TOKENS = 512
SPAN = 256
RANKS = 128
PROMPT_TOKENS = 65536


def draw_queries(key, part):
    tensor_shape = (PROMPT_TOKENS, QUERY_HEADS * HEAD_SIZE)
    base_offset = 1.5 * jax.random.normal(jax.random.fold_in(key, 1), tensor_shape, jnp.float32)
    return jnp.clip(base_offset, -9.0, 9.0).astype(jnp.bfloat16)


def draw_keys(key, part):
    tensor_shape = (PROMPT_TOKENS, KEY_VALUE_HEADS * HEAD_SIZE)
    base_offset = jax.random.normal(jax.random.fold_in(key, 2), tensor_shape, jnp.float32)
    return jnp.clip(base_offset, -6.0, 6.0).astype(jnp.bfloat16)


def draw_positions(key, part):
    order = jnp.arange(PROMPT_TOKENS, dtype=jnp.int32)
    halfway = PROMPT_TOKENS // 2
    flags = jax.random.randint(jax.random.fold_in(key, 3), (PROMPT_TOKENS,), 0, max(PROMPT_TOKENS // 3, 2)) == 0
    flags = flags & (order < halfway) | (order == 0) | (order == halfway)
    begins = lax.cummax(jnp.where(flags, order, 0).astype(jnp.int32), axis=0)
    natural = (order - begins).astype(jnp.int32)
    block_of = order // BLOCK_TOKENS
    offset = order % BLOCK_TOKENS
    sequence_at = jnp.where(offset < SPAN, block_of * SPAN + offset, (2 * RANKS - 1 - block_of) * SPAN + offset - SPAN).astype(jnp.int32)
    return jnp.take(natural, sequence_at, axis=0).astype(jnp.int32)


def steps_of(own_key, extent, pieces, low, top_value):
    loudness = 1.0
    for axis_at, parts in pieces:
        steps = jax.random.uniform(jax.random.fold_in(jax.random.fold_in(own_key, 6), axis_at), (parts,), jnp.float32, low / len(pieces), top_value / len(pieces))
        loudness = loudness * jnp.repeat(jnp.exp(steps), extent[axis_at] // parts).reshape((-1,) + (1,) * (len(extent) - 1 - axis_at))
    return loudness


def gaussian(key, shape, scale, bound, pieces=(), kind=jnp.bfloat16):
    loudness = steps_of(key, shape, pieces, -0.22, 0.18) if pieces else 1.0
    entries = jax.random.normal(key, shape, jnp.float32) * scale * loudness
    return jnp.minimum(jnp.maximum(entries, -bound), bound).astype(kind)


def setup_inputs(seed: int = 0) -> dict:
    key_list = jax.random.split(jax.random.key(seed), 6)
    return {
        "queries": draw_queries(jax.random.fold_in(key_list[5], 71), 0),
        "keys": draw_keys(jax.random.fold_in(key_list[5], 71), 0),
        "values": gaussian(key_list[2], (PROMPT_TOKENS, KEY_VALUE_HEADS * HEAD_SIZE), 4.0, 24.0, ((0, 128), (1, 2))),
        "positions": draw_positions(jax.random.fold_in(key_list[5], 71), 0),
        "out_weight": gaussian(key_list[4], (QUERY_HEADS * HEAD_SIZE, D), (QUERY_HEADS * HEAD_SIZE) ** -0.5, 0.125, ((1, 2),)),
    }


neg_large = -1e+30

def rotate(block, positions, width):
    halfway = width // 2
    table = np.power(500000.0, -2.0 * np.arange(halfway) / width).astype(np.float32)
    angle = positions.astype(jnp.float32)[:, None] * jnp.asarray(table, dtype=jnp.float32)[None, :]
    cosine = jnp.cos(angle)[:, None, :]
    sinus = jnp.sin(angle)[:, None, :]
    number = block.shape[0]
    groups = block.shape[1] // width
    split_up = block.astype(jnp.float32).reshape(number, groups, width)
    leading = split_up[:, :, :halfway]
    trailing = split_up[:, :, halfway:]
    turned = jnp.concatenate([leading * cosine - trailing * sinus, trailing * cosine + leading * sinus], axis=2)
    return turned.reshape(number, groups * width).astype(jnp.bfloat16)

def reference(queries, keys, values, positions, out_weight):
    within = jnp.arange(PROMPT_TOKENS, dtype=jnp.int32)
    block_of = within // BLOCK_TOKENS
    offset = within % BLOCK_TOKENS
    index_of = jnp.where(offset < SPAN, block_of * SPAN + offset, (2 * RANKS - 1 - block_of) * SPAN + offset - SPAN).astype(jnp.int32)
    doc_start = (index_of - positions).astype(jnp.int32)
    q_rot = rotate(queries, positions, HEAD_SIZE)
    rotary_keys = rotate(keys, positions, HEAD_SIZE)
    query_group = QUERY_HEADS // KEY_VALUE_HEADS
    scale = 1.0 / math.sqrt(HEAD_SIZE)

    def one_block(number):
        first_row = (number * BLOCK_TOKENS).astype(jnp.int32)
        query_row_slice = lax.dynamic_slice_in_dim(q_rot, first_row, BLOCK_TOKENS, 0)
        query_index = lax.dynamic_slice_in_dim(index_of, first_row, BLOCK_TOKENS, 0)
        query_start = lax.dynamic_slice_in_dim(doc_start, first_row, BLOCK_TOKENS, 0)
        sources = ((number - jnp.arange(STEPS, dtype=jnp.int32)) % RANKS).astype(jnp.int32)
        key_row_slice = (sources[:, None] * BLOCK_TOKENS + jnp.arange(BLOCK_TOKENS, dtype=jnp.int32)[None, :]).reshape(-1)
        key_tile_block = jnp.take(rotary_keys, key_row_slice, axis=0).astype(jnp.float32).reshape(-1, KEY_VALUE_HEADS, HEAD_SIZE)
        value_tile_block = jnp.take(values, key_row_slice, axis=0).astype(jnp.float32).reshape(-1, KEY_VALUE_HEADS, HEAD_SIZE)
        key_index = jnp.take(index_of, key_row_slice, axis=0)
        query_float_rows = query_row_slice.astype(jnp.float32).reshape(BLOCK_TOKENS, KEY_VALUE_HEADS, query_group, HEAD_SIZE)
        scores = jnp.einsum('qhgd,khd->hgqk', query_float_rows, key_tile_block, precision=lax.Precision.HIGHEST) * scale
        allowed = (key_index[None, :] <= query_index[:, None]) & (key_index[None, :] >= query_start[:, None])
        scores = jnp.where(allowed, scores, neg_large)
        highest = lax.optimization_barrier(jnp.max(scores, axis=3, keepdims=True))
        weights = jnp.where(allowed, jnp.exp(scores - highest), 0.0)
        total = lax.optimization_barrier(jnp.sum(weights, axis=3))
        rounded = lax.optimization_barrier(weights.astype(jnp.bfloat16)).astype(jnp.float32)
        summed = jnp.einsum('hgqk,khd->qhgd', rounded, value_tile_block, precision=lax.Precision.HIGHEST)
        result = summed / jnp.transpose(total, (2, 0, 1))[..., None]
        return result.reshape(BLOCK_TOKENS, QUERY_HEADS * HEAD_SIZE).astype(jnp.bfloat16)
    attended = lax.map(one_block, jnp.arange(RANKS, dtype=jnp.int32)).reshape(PROMPT_TOKENS, QUERY_HEADS * HEAD_SIZE)
    return jnp.dot(attended, out_weight, preferred_element_type=jnp.float32).astype(jnp.bfloat16)
```

```python
import functools
import math

import jax
import jax.numpy as jnp
import numpy as np
from jax import lax
from jax.experimental import pallas as pl
from jax.experimental.pallas import tpu as pltpu
from jax.sharding import PartitionSpec as P

HEAD = 128
STEPS = 4
MASKED = -1e30
MESH = pl.DeviceIdType.MESH

PART_1 = 1.5703125
PART_2 = 507.0 / 2.0**20
PART_3 = math.pi / 2 - PART_1 - PART_2


def cosine_and_sine(angle, lane):
    turns = jnp.floor(angle * (2.0 / math.pi) + 0.5)
    rest = ((angle - turns * PART_1) - turns * PART_2) - turns * PART_3
    quadrant = turns.astype(jnp.int32) + jnp.where(lane < HEAD // 2, 1, 0)
    z = rest * rest
    sine = ((-1.9515295891e-4 * z + 8.3321608736e-3) * z - 1.6666654611e-1) * z * rest + rest
    cosine = ((2.443315711809948e-5 * z - 1.388731625493765e-3) * z + 4.166664568298827e-2) * z * z - 0.5 * z + 1.0
    value = jnp.where((quadrant & 1) == 1, cosine, sine)
    return jnp.where((quadrant & 2) == 2, -value, value)


def kernel(
    cycle,
    q_hbm, k_hbm, v_hbm, pos_hbm, freq_hbm, w_hbm,
    out_ref,
    q_in, k_in, v_in, pos_in, freq_in, weight,
    pos_col, cos_tab, sin_tab, q_rot, own_kv, met_kv, top, total, sums, att_own, att_met, mixed,
    load_sem, kv_send, kv_recv, x_send, x_recv,
):
    block = lax.axis_index("ctx")
    head = lax.axis_index("head")
    half = q_in.shape[1] // 2
    pairs = q_in.shape[0]
    groups = own_kv.shape[1]
    wide = 2 * HEAD
    scale = math.log2(math.e) / math.sqrt(HEAD)
    even = lax.rem(block, 2) == 0
    twin = jnp.where(even, block + 1, block - 1)

    small = [
        pltpu.make_async_copy(pos_hbm, pos_in, load_sem.at[0]),
        pltpu.make_async_copy(freq_hbm, freq_in, load_sem.at[1]),
        pltpu.make_async_copy(k_hbm, k_in, load_sem.at[2]),
        pltpu.make_async_copy(v_hbm, v_in, load_sem.at[3]),
    ]
    for copy in small:
        copy.start()
    q_loads = [
        pltpu.make_async_copy(q_hbm.at[:, pl.ds(p * wide, wide)], q_in.at[p], load_sem.at[4 + p]) for p in range(pairs)
    ]
    for copy in q_loads:
        copy.start()
    rows = weight.shape[1]
    w_loads = [
        pltpu.make_async_copy(w_hbm.at[pl.ds(pl.multiple_of(head * rows, rows), rows)], weight.at[0], load_sem.at[8]),
        pltpu.make_async_copy(
            w_hbm.at[pl.ds(pl.multiple_of((1 - head) * rows, rows), rows)], weight.at[1], load_sem.at[9]
        ),
    ]
    for copy in w_loads:
        copy.start()

    def at(step):
        return (lax.rem(block + step + cycle, cycle), head)

    barrier = pltpu.get_barrier_semaphore()
    friends = [at(1), at(-1), at(3), at(-3), (block, 1 - head), (twin, head)]
    for friend in friends:
        pl.semaphore_signal(barrier, inc=1, device_id=friend, device_id_type=MESH)

    for copy in small:
        copy.wait()
    lane = lax.broadcasted_iota(jnp.int32, (HEAD, HEAD), 1)
    frequency = freq_in[0:1, :]
    for i in range(2 * half // HEAD):
        cut = pl.ds(i * HEAD, HEAD)
        column = jnp.transpose(jnp.broadcast_to(pos_in[i : i + 1, :].astype(jnp.float32), (HEAD, HEAD)))
        pos_col[cut, :] = column.astype(jnp.int32)
        both = cosine_and_sine(column * frequency, lane)
        other = pltpu.roll(both, HEAD // 2, 1)
        cos_tab[cut, :] = jnp.where(lane < HEAD // 2, both, other)
        sin_tab[cut, :] = jnp.where(lane < HEAD // 2, -other, both)

    def rotated(block_rows, cut):
        value = block_rows.astype(jnp.float32)
        return (value * cos_tab[cut, :] + pltpu.roll(value, HEAD // 2, 1) * sin_tab[cut, :]).astype(jnp.bfloat16)

    for part in range(2):
        cut = pl.ds(part * half, half)
        for group in range(groups):
            columns = pl.ds(group * HEAD, HEAD)
            own_kv[part, group, 0] = rotated(k_in[cut, columns], cut)
            own_kv[part, group, 1] = v_in[cut, columns]

    pl.semaphore_wait(barrier, len(friends))

    def kv_copy(slot, step, group):
        part = jnp.where(block + step < cycle, 0, 1)
        return pltpu.make_async_remote_copy(
            own_kv.at[part, group], met_kv.at[step - 1, group], kv_send.at[slot, group], kv_recv.at[step - 1, group],
            device_id=at(step), device_id_type=MESH,
        )

    first_step = jnp.where(even, 1, 3)
    other_step = 4 - first_step

    def hand_copy(group):
        return pltpu.make_async_remote_copy(
            met_kv.at[first_step - 1, group], met_kv.at[1, group], kv_send.at[2, group], kv_recv.at[1, group],
            device_id=(twin, head), device_id_type=MESH,
        )

    def kv_wait(step, group):
        pltpu.make_async_remote_copy(
            met_kv.at[step - 1, group], met_kv.at[step - 1, group], kv_send.at[2, group], kv_recv.at[step - 1, group],
            device_id=(twin, head), device_id_type=MESH,
        ).wait_recv()

    for group in range(groups):
        kv_copy(0, 1, group).start()
        kv_copy(1, 3, group).start()

    def x_copy(part, order, p):
        cut = pl.ds(pl.multiple_of(part * half, half), half)
        return pltpu.make_async_remote_copy(
            att_own.at[p, cut], att_met.at[p, cut], x_send.at[order, p], x_recv.at[order, p],
            device_id=(block, 1 - head), device_id_type=MESH,
        )

    first = jnp.where(block == 0, 0, 1)
    second = 1 - first
    mixing = (block == 1) | (block == 2)

    row_at = lax.broadcasted_iota(jnp.int32, (half, wide), 0)
    key_at = lax.broadcasted_iota(jnp.int32, (half, wide), 1)

    def both_lanes(value):
        return jnp.concatenate([value, value], axis=1)

    def finish(part, p):
        cut = pl.ds(pl.multiple_of(part * half, half), half)
        for i in range(2):
            sum_all = jnp.sum(total[2 * p + i, cut, :], axis=1, keepdims=True)
            att_own[p, cut, i * HEAD : (i + 1) * HEAD] = (sums[2 * p + i, cut, :] / sum_all).astype(jnp.bfloat16)

    for copy in q_loads:
        copy.wait()

    def own_block(i, carry):
        part = jnp.where(i < pairs, first, second)
        p = lax.rem(i, pairs)
        cut = pl.ds(pl.multiple_of(part * half, half), half)
        group = p // (pairs // groups)
        keys = own_kv[part, group, 0]
        values = own_kv[part, group, 1]
        reach = both_lanes(pos_col[cut, :])
        seen = (key_at <= row_at) & (key_at >= row_at - reach)
        for n in range(2):
            query = rotated(q_in[p, cut, n * HEAD : (n + 1) * HEAD], cut)
            q_rot[p, cut, n * HEAD : (n + 1) * HEAD] = query
            scores = lax.dot_general(query, keys, (((1,), (1,)), ((), ())), preferred_element_type=jnp.float32)
            scores = jnp.where(seen, scores, MASKED)
            highest = jnp.broadcast_to(jnp.max(scores, axis=1, keepdims=True), (half, HEAD))
            weights = jnp.exp2((scores - both_lanes(highest)) * scale)
            top[2 * p + n, cut, :] = highest
            total[2 * p + n, cut, :] = weights[:, :HEAD] + weights[:, HEAD:]
            sums[2 * p + n, cut, :] = jnp.dot(
                weights.astype(jnp.bfloat16), values, preferred_element_type=jnp.float32
            )

        @pl.when((i < pairs) & jnp.logical_not(mixing))
        def _():
            finish(part, p)
            x_copy(part, 0, p).start()

        return carry

    lax.fori_loop(0, 2 * pairs, own_block, 0)

    def met_block(step, group, p):
        early = step <= block
        part = jnp.where(early, 0, 1)
        apart = jnp.where(early, step, cycle - step) * half
        cut = pl.ds(pl.multiple_of(part * half, half), half)
        keys = met_kv[step - 1, group, 0]
        values = met_kv[step - 1, group, 1]
        reach = both_lanes(pos_col[cut, :])
        seen = key_at >= row_at - reach + apart
        for n in range(2):
            query = q_rot[p, cut, n * HEAD : (n + 1) * HEAD]
            scores = lax.dot_general(query, keys, (((1,), (1,)), ((), ())), preferred_element_type=jnp.float32)
            scores = jnp.where(seen, scores, MASKED)
            before = top[2 * p + n, cut, :]
            highest = jnp.maximum(before, jnp.max(scores, axis=1, keepdims=True))
            factor = jnp.exp2((before - highest) * scale)
            weights = jnp.exp2((scores - both_lanes(highest)) * scale)
            top[2 * p + n, cut, :] = highest
            total[2 * p + n, cut, :] = total[2 * p + n, cut, :] * factor + (weights[:, :HEAD] + weights[:, HEAD:])
            sums[2 * p + n, cut, :] = sums[2 * p + n, cut, :] * factor + jnp.dot(
                weights.astype(jnp.bfloat16), values, preferred_element_type=jnp.float32
            )

    tile = 512
    tiles = out_ref.shape[1] // tile

    def project(att, which, part, begin, end, fresh, last):
        cut = pl.ds(pl.multiple_of(part * half, half), half)
        row_cut = slice(begin * wide, end * wide)

        def one(t, carry):
            columns = pl.ds(pl.multiple_of(t * tile, tile), tile)
            left = jnp.concatenate([att[p, cut, :] for p in range(begin, end)], axis=1)
            value = jnp.dot(left, weight[which, row_cut, columns], preferred_element_type=jnp.float32)
            if not fresh:
                value = mixed[cut, columns] + value
            if last:
                out_ref[cut, columns] = value.astype(jnp.bfloat16)
            else:
                mixed[cut, columns] = value
            return carry

        lax.fori_loop(0, tiles, one, 0)

    per_group = pairs // groups

    def met_group(group):
        for step, known in ((first_step, True), (other_step, False), (2, False)):
            if not known:
                kv_wait(step, group)

            def one(p, carry):
                met_block(step, group, group * per_group + p)
                return carry

            lax.fori_loop(0, per_group, one, 0)
        for p in range(group * per_group, (group + 1) * per_group):
            finish(second, p)
            x_copy(second, 1, p).start()

            @pl.when(mixing)
            def _():
                finish(first, p)
                x_copy(first, 0, p).start()

    kv_wait(first_step, 0)
    hand_copy(0).start()
    met_group(0)
    kv_wait(first_step, 1)
    hand_copy(1).start()
    met_group(1)

    for copy in w_loads:
        copy.wait()
    project(att_own, 0, first, 0, pairs, True, False)
    project(att_own, 0, second, 0, pairs, True, False)
    for p in range(pairs):
        x_copy(first, 0, p).wait_recv()
    project(att_met, 1, first, 0, pairs, False, True)
    for p in range(pairs - 1):
        x_copy(second, 1, p).wait_recv()
    project(att_met, 1, second, 0, pairs - 1, False, False)
    x_copy(second, 1, pairs - 1).wait_recv()
    project(att_met, 1, second, pairs - 1, pairs, False, True)

    for p in range(pairs):
        x_copy(first, 0, p).wait_send()
        x_copy(second, 1, p).wait_send()
    for group in range(groups):
        kv_copy(0, 1, group).wait_send()
        kv_copy(1, 3, group).wait_send()
        hand_copy(group).wait_send()


def shards(queries, keys, values, positions, out_weight):
    number, width = queries.shape
    half = number // 2
    pairs = width // (2 * HEAD)
    groups = keys.shape[1] // HEAD
    heads = width // HEAD
    columns = out_weight.shape[1]
    cycle = lax.axis_size("ctx")
    table = np.power(500000.0, -2.0 * np.arange(HEAD // 2) / HEAD).astype(np.float32)
    frequency = jnp.asarray(np.tile(np.concatenate([table, table])[None, :], (8, 1)))
    f32, bf16, i32 = jnp.float32, jnp.bfloat16, jnp.int32
    hbm = pl.BlockSpec(memory_space=pltpu.MemorySpace.HBM)
    return pl.pallas_call(
        functools.partial(kernel, cycle),
        name="attend_and_project",
        out_shape=jax.ShapeDtypeStruct((number, columns), bf16),
        in_specs=[hbm] * 6,
        out_specs=pl.BlockSpec(memory_space=pltpu.MemorySpace.VMEM),
        scratch_shapes=[
            pltpu.VMEM((pairs, number, 2 * HEAD), bf16),
            pltpu.VMEM((number, groups * HEAD), bf16),
            pltpu.VMEM((number, groups * HEAD), bf16),
            pltpu.VMEM((number // HEAD, HEAD), i32),
            pltpu.VMEM((8, HEAD), f32),
            pltpu.VMEM((2, width, columns), bf16),
            pltpu.VMEM((number, HEAD), i32),
            pltpu.VMEM((number, HEAD), f32),
            pltpu.VMEM((number, HEAD), f32),
            pltpu.VMEM((pairs, number, 2 * HEAD), bf16),
            pltpu.VMEM((2, groups, 2, half, HEAD), bf16),
            pltpu.VMEM((STEPS - 1, groups, 2, half, HEAD), bf16),
            pltpu.VMEM((heads, number, HEAD), f32),
            pltpu.VMEM((heads, number, HEAD), f32),
            pltpu.VMEM((heads, number, HEAD), f32),
            pltpu.VMEM((pairs, number, 2 * HEAD), bf16),
            pltpu.VMEM((pairs, number, 2 * HEAD), bf16),
            pltpu.VMEM((number, columns), f32),
            pltpu.SemaphoreType.DMA((10,)),
            pltpu.SemaphoreType.DMA((STEPS - 1, groups)),
            pltpu.SemaphoreType.DMA((STEPS - 1, groups)),
            pltpu.SemaphoreType.DMA((2, pairs)),
            pltpu.SemaphoreType.DMA((2, pairs)),
        ],
        compiler_params=pltpu.CompilerParams(collective_id=0, has_side_effects=True, vmem_limit_bytes=61 << 20),
    )(queries, keys, values, positions.reshape(number // HEAD, HEAD), frequency, out_weight)


def solution(mesh):
    in_specs = (P("ctx", "head"), P("ctx", "head"), P("ctx", "head"), P("ctx"), P(None, "head"))
    out_specs = P("ctx", "head")
    return jax.shard_map(shards, mesh=mesh, in_specs=in_specs, out_specs=out_specs, check_vma=False)
```

```python
import functools
import math

import jax
import jax.numpy as jnp
import numpy as np
from jax import lax
from jax.experimental import pallas as pl
from jax.experimental.pallas import tpu as pltpu
from jax.sharding import PartitionSpec as P

HEAD = 128
STEPS = 4
MASKED = -1e30
MESH = pl.DeviceIdType.MESH

PART_1 = 1.5703125
PART_2 = 507.0 / 2.0**20
PART_3 = math.pi / 2 - PART_1 - PART_2


def cosine_and_sine(angle, lane):
    turns = jnp.floor(angle * (2.0 / math.pi) + 0.5)
    rest = ((angle - turns * PART_1) - turns * PART_2) - turns * PART_3
    quadrant = turns.astype(jnp.int32) + jnp.where(lane < HEAD // 2, 1, 0)
    z = rest * rest
    sine = ((-1.9515295891e-4 * z + 8.3321608736e-3) * z - 1.6666654611e-1) * z * rest + rest
    cosine = ((2.443315711809948e-5 * z - 1.388731625493765e-3) * z + 4.166664568298827e-2) * z * z - 0.5 * z + 1.0
    value = jnp.where((quadrant & 1) == 1, cosine, sine)
    return jnp.where((quadrant & 2) == 2, -value, value)


def kernel(
    cycle,
    q_hbm, k_hbm, v_hbm, pos_hbm, freq_hbm, w_hbm,
    out_ref,
    q_in, k_in, v_in, pos_in, freq_in, weight,
    pos_col, cos_tab, sin_tab, q_rot, own_k, own_v, met_k, met_v, top, total, sums, att_own, att_met, mixed,
    load_sem, kv_send, kv_recv, x_send, x_recv,
):
    block = lax.axis_index("ctx")
    head = lax.axis_index("head")
    half = q_in.shape[1] // 2
    pairs = q_in.shape[0]
    groups = own_k.shape[1]
    wide = 2 * HEAD
    scale = math.log2(math.e) / math.sqrt(HEAD)
    even = lax.rem(block, 2) == 0
    twin = jnp.where(even, block + 1, block - 1)

    small = [
        pltpu.make_async_copy(pos_hbm, pos_in, load_sem.at[0]),
        pltpu.make_async_copy(freq_hbm, freq_in, load_sem.at[1]),
        pltpu.make_async_copy(k_hbm, k_in, load_sem.at[2]),
        pltpu.make_async_copy(v_hbm, v_in, load_sem.at[3]),
    ]
    for copy in small:
        copy.start()
    q_loads = [
        pltpu.make_async_copy(q_hbm.at[:, pl.ds(p * wide, wide)], q_in.at[p], load_sem.at[4 + p]) for p in range(pairs)
    ]
    for copy in q_loads:
        copy.start()
    rows = weight.shape[1]
    w_loads = [
        pltpu.make_async_copy(w_hbm.at[pl.ds(pl.multiple_of(head * rows, rows), rows)], weight.at[0], load_sem.at[8]),
        pltpu.make_async_copy(
            w_hbm.at[pl.ds(pl.multiple_of((1 - head) * rows, rows), rows)], weight.at[1], load_sem.at[9]
        ),
    ]

    def at(step):
        return (lax.rem(block + step + cycle, cycle), head)

    place = lax.rem(block, 8)
    last = {1: (place == 7) & (block < cycle - 1), 3: place == 7}
    relay = ((place == 1) & (block + 7 < cycle)) | (place == 3)
    origin = at(jnp.where(place == 1, 6, 4))

    def goal(step):
        return at(jnp.where(last[step], step - 7, step))

    barrier = pltpu.get_barrier_semaphore()
    senders = [
        at(jnp.where((place == 0) & (block > 0), -7, -1)), at(jnp.where(place == 2, -7, -3)), (block, 1 - head), (twin, head),
    ]
    for friend in senders:
        pl.semaphore_signal(barrier, inc=1, device_id=friend, device_id_type=MESH)

    @pl.when(relay)
    def _():
        pl.semaphore_signal(barrier, inc=1, device_id=origin, device_id_type=MESH)

    VALUES = groups

    def own_piece(part, piece):
        return own_k.at[part, piece] if piece < VALUES else own_v.at[part]

    def met_piece(slot, piece):
        return met_k.at[slot, piece] if piece < VALUES else met_v.at[slot]

    def kv_copy(slot, step, piece):
        part = jnp.where(block + step < cycle, 0, 1)
        there = jnp.where(last[step], STEPS - 1, step - 1)
        return pltpu.make_async_remote_copy(
            own_piece(part, piece), met_piece(there, piece), kv_send.at[slot, piece], kv_recv.at[there, piece],
            device_id=goal(step), device_id_type=MESH,
        )

    def kv_start(piece):
        kv_copy(0, 1, piece).start()
        kv_copy(1, 3, piece).start()

    first_step = jnp.where(even, 1, 3)
    other_step = 4 - first_step

    def hand_copy(piece):
        return pltpu.make_async_remote_copy(
            met_piece(first_step - 1, piece), met_piece(1, piece), kv_send.at[2, piece], kv_recv.at[1, piece],
            device_id=(twin, head), device_id_type=MESH,
        )

    def relay_copy(piece):
        there = jnp.where(place == 1, 0, 2)
        return pltpu.make_async_remote_copy(
            met_piece(STEPS - 1, piece), met_piece(there, piece), kv_send.at[3, piece], kv_recv.at[there, piece],
            device_id=at(7), device_id_type=MESH,
        )

    def kv_wait(slot, piece):
        pltpu.make_async_remote_copy(
            met_piece(slot, piece), met_piece(slot, piece), kv_send.at[2, piece], kv_recv.at[slot, piece],
            device_id=(twin, head), device_id_type=MESH,
        ).wait_recv()

    for copy in small[3:]:
        copy.wait()
    for part in range(2):
        for group in range(groups):
            own_v[part, group] = v_in[pl.ds(part * half, half), pl.ds(group * HEAD, HEAD)]
    pl.semaphore_wait(barrier, jnp.where(relay, 5, 4))
    kv_start(VALUES)

    for copy in small[:3]:
        copy.wait()
    lane = lax.broadcasted_iota(jnp.int32, (HEAD, HEAD), 1)
    frequency = freq_in[0:1, :]

    def rotated(block_rows, cut):
        value = block_rows.astype(jnp.float32)
        return (value * cos_tab[cut, :] + pltpu.roll(value, HEAD // 2, 1) * sin_tab[cut, :]).astype(jnp.bfloat16)

    def prepare(part):
        for i in range(half // HEAD):
            cut = pl.ds(pl.multiple_of(part * half + i * HEAD, HEAD), HEAD)
            line = pos_in[pl.ds(part * (half // HEAD) + i, 1), :].astype(jnp.float32)
            column = jnp.transpose(jnp.broadcast_to(line, (HEAD, HEAD)))
            pos_col[cut, :] = column.astype(jnp.int32)
            both = cosine_and_sine(column * frequency, lane)
            other = pltpu.roll(both, HEAD // 2, 1)
            cos_tab[cut, :] = jnp.where(lane < HEAD // 2, both, other)
            sin_tab[cut, :] = jnp.where(lane < HEAD // 2, -other, both)
        cut = pl.ds(pl.multiple_of(part * half, half), half)
        for group in range(groups):
            own_k[part, group] = rotated(k_in[cut, pl.ds(group * HEAD, HEAD)], cut)

    def x_copy(part, order, p):
        cut = pl.ds(pl.multiple_of(part * half, half), half)
        return pltpu.make_async_remote_copy(
            att_own.at[p, cut], att_met.at[p, cut], x_send.at[order, p], x_recv.at[order, p],
            device_id=(block, 1 - head), device_id_type=MESH,
        )

    far = block < STEPS - 1

    first = jnp.where(far, 0, 1)
    second = 1 - first
    alone = jnp.logical_not(far) | (block == 0)

    row_at = lax.broadcasted_iota(jnp.int32, (half, wide), 0)
    key_at = lax.broadcasted_iota(jnp.int32, (half, wide), 1)
    per_group = pairs // groups

    def both_lanes(value):
        return jnp.concatenate([value, value], axis=1)

    def finish(part, p):
        cut = pl.ds(pl.multiple_of(part * half, half), half)
        for n in range(2):
            share = 1.0 / jnp.sum(total[2 * p + n, cut, :], axis=1, keepdims=True)
            att_own[p, cut, n * HEAD : (n + 1) * HEAD] = (sums[2 * p + n, cut, :] * share).astype(jnp.bfloat16)

    def own_block(part, p):
        cut = pl.ds(pl.multiple_of(part * half, half), half)
        group = p // per_group
        keys = own_k[part, group]
        values = own_v[part, group]
        reach = both_lanes(pos_col[cut, :])
        seen = (key_at <= row_at) & (key_at >= row_at - reach)
        for m in range(2):
            lanes = slice(m * HEAD, (m + 1) * HEAD)
            h = 2 * p + m
            query = rotated(q_in[p, cut, lanes], cut)
            q_rot[p, cut, lanes] = query
            scores = lax.dot_general(query, keys, (((1,), (1,)), ((), ())), preferred_element_type=jnp.float32)
            scores = jnp.where(seen, scores, MASKED)
            highest = jnp.broadcast_to(jnp.max(scores, axis=1, keepdims=True), (half, HEAD))
            weights = jnp.exp2((scores - both_lanes(highest)) * scale)
            top[h, cut, :] = highest
            total[h, cut, :] = weights[:, :HEAD] + weights[:, HEAD:]
            sums[h, cut, :] = jnp.dot(weights.astype(jnp.bfloat16), values, preferred_element_type=jnp.float32)

    def first_own(p, carry):
        own_block(first, p)

        @pl.when(alone)
        def _():
            finish(first, p)
            x_copy(first, 0, p).start()

        @pl.when(p == 0)
        def _():
            prepare(second)
            for piece in range(groups):
                kv_start(piece)

        @pl.when(relay & (p == 1))
        def _():
            for piece in (VALUES, *range(groups)):
                kv_wait(STEPS - 1, piece)
                relay_copy(piece).start()

        return carry

    def second_own(group, carry):
        for m in range(per_group):
            own_block(second, group * per_group + m)
        return carry

    prepare(first)
    for copy in q_loads:
        copy.wait()
    for copy in w_loads:
        copy.start()
    lax.fori_loop(0, pairs, first_own, 0)
    lax.fori_loop(0, groups, second_own, 0)

    def met_block(step, group):
        early = step <= block
        part = jnp.where(early, 0, 1)
        apart = jnp.where(early, step, cycle - step) * half
        cut = pl.ds(pl.multiple_of(part * half, half), half)
        keys = met_k[step - 1, group]
        values = met_v[step - 1, group]
        reach = both_lanes(pos_col[cut, :])
        seen = key_at >= row_at - reach + apart
        for m in range(2 * per_group):
            p = group * per_group + m // 2
            lanes = slice((m % 2) * HEAD, (m % 2 + 1) * HEAD)
            h = 2 * group * per_group + m
            query = q_rot[p, cut, lanes]
            scores = lax.dot_general(query, keys, (((1,), (1,)), ((), ())), preferred_element_type=jnp.float32)
            scores = jnp.where(seen, scores, MASKED)
            before = top[h, cut, :]
            highest = jnp.maximum(before, jnp.max(scores, axis=1, keepdims=True))
            factor = jnp.exp2((before - highest) * scale)
            weights = jnp.exp2((scores - both_lanes(highest)) * scale)
            top[h, cut, :] = highest
            total[h, cut, :] = total[h, cut, :] * factor + (weights[:, :HEAD] + weights[:, HEAD:])
            sums[h, cut, :] = sums[h, cut, :] * factor + jnp.dot(
                weights.astype(jnp.bfloat16), values, preferred_element_type=jnp.float32
            )
        return part

    def pick(i, usual, one, two):
        def listed(values):
            value = jnp.int32(values[-1])
            for n in range(len(values) - 1):
                value = jnp.where(i == n, values[n], value)
            return value

        return jnp.where(block == 1, listed(one), jnp.where(block == 2, listed(two), listed(usual)))

    usual_steps = (
        jnp.where(place == 0, other_step, first_step),
        jnp.where(place == 0, first_step, jnp.where(place == 2, 2, other_step)),
        jnp.where(place == 2, other_step, 2),
    )

    def meeting(i, carry):
        group = pick(i, (0, 0, 0, 1, 1, 1), (0, 1, 0, 0, 1, 1), (0, 0, 1, 1, 0, 1))
        turn = pick(i, (-1, -2, -3, -1, -2, -3), (1, 1, 3, 2, 3, 2), (1, 2, 1, 2, 3, 3))
        step = turn
        for n in range(STEPS - 1):
            step = jnp.where(turn == -1 - n, usual_steps[n], step)
        done = pick(i, (0, 0, 1, 0, 0, 1), (1, 1, 0, 1, 0, 1), (0, 1, 0, 1, 1, 1))
        handing = step == first_step

        def arrive(piece):
            kv_wait(step - 1, piece)
            pl.when(handing)(lambda: hand_copy(piece).start())

        for known in range(groups):
            pl.when(group == known)(lambda: arrive(known))
        pl.when(group == 0)(lambda: arrive(VALUES))
        part = met_block(step, group)

        @pl.when(done == 1)
        def _():
            for m in range(per_group):
                p = group * per_group + m
                finish(part, p)
                x_copy(part, jnp.where(part == first, 0, 1), p).start()

        return carry

    lax.fori_loop(0, 2 * (STEPS - 1), meeting, 0)

    tile = 256
    tiles = out_ref.shape[1] // tile

    def project(part, own, met, fresh, last):
        cut = pl.ds(pl.multiple_of(part * half, half), half)

        for t in range(tiles):
            columns = slice(t * tile, (t + 1) * tile)
            value = None if fresh else mixed[cut, columns]
            for which, att, (begin, end) in ((0, att_own, own), (1, att_met, met)):
                if begin < end:
                    left = jnp.concatenate([att[p, cut, :] for p in range(begin, end)], axis=1)
                    right = weight[which, begin * wide : end * wide, columns]
                    more = jnp.dot(left, right, preferred_element_type=jnp.float32)
                    value = more if value is None else value + more
            if last:
                out_ref[cut, columns] = value.astype(jnp.bfloat16)
            else:
                mixed[cut, columns] = value

    for copy in w_loads:
        copy.wait()
    for p in range(pairs):
        x_copy(first, 0, p).wait_recv()
    project(first, (0, pairs), (0, pairs), True, True)
    for p in range(per_group):
        x_copy(second, 1, p).wait_recv()
    project(second, (0, pairs), (0, per_group), True, False)
    for p in range(per_group, pairs):
        x_copy(second, 1, p).wait_recv()
        project(second, (0, 0), (p, p + 1), False, p == pairs - 1)

    for p in range(pairs):
        x_copy(first, 0, p).wait_send()
        x_copy(second, 1, p).wait_send()
    for piece in range(groups + 1):
        kv_copy(0, 1, piece).wait_send()
        kv_copy(1, 3, piece).wait_send()
        hand_copy(piece).wait_send()

    @pl.when(relay)
    def _():
        for piece in range(groups + 1):
            relay_copy(piece).wait_send()


def store(value_ref, out_hbm, sem):
    rows = value_ref.shape[0] // sem.shape[0]
    copies = [
        pltpu.make_async_copy(value_ref.at[pl.ds(i * rows, rows)], out_hbm.at[pl.ds(i * rows, rows)], sem.at[i])
        for i in range(sem.shape[0])
    ]
    for copy in copies:
        copy.start()
    for copy in copies:
        copy.wait()


def shards(queries, keys, values, positions, out_weight):
    number, width = queries.shape
    half = number // 2
    pairs = width // (2 * HEAD)
    groups = keys.shape[1] // HEAD
    heads = width // HEAD
    columns = out_weight.shape[1]
    cycle = lax.axis_size("ctx")
    table = np.power(500000.0, -2.0 * np.arange(HEAD // 2) / HEAD).astype(np.float32)
    frequency = jnp.asarray(np.tile(np.concatenate([table, table])[None, :], (8, 1)))
    f32, bf16, i32 = jnp.float32, jnp.bfloat16, jnp.int32
    hbm = pl.BlockSpec(memory_space=pltpu.MemorySpace.HBM)
    projected = pl.pallas_call(
        functools.partial(kernel, cycle),
        name="attend_and_project",
        out_shape=pltpu.VMEM((number, columns), bf16),
        in_specs=[hbm] * 6,
        out_specs=pl.BlockSpec(memory_space=pltpu.MemorySpace.VMEM),
        scratch_shapes=[
            pltpu.VMEM((pairs, number, 2 * HEAD), bf16),
            pltpu.VMEM((number, groups * HEAD), bf16),
            pltpu.VMEM((number, groups * HEAD), bf16),
            pltpu.VMEM((number // HEAD, HEAD), i32),
            pltpu.VMEM((8, HEAD), f32),
            pltpu.VMEM((2, width, columns), bf16),
            pltpu.VMEM((number, HEAD), i32),
            pltpu.VMEM((number, HEAD), f32),
            pltpu.VMEM((number, HEAD), f32),
            pltpu.VMEM((pairs, number, 2 * HEAD), bf16),
            pltpu.VMEM((2, groups, half, HEAD), bf16),
            pltpu.VMEM((2, groups, half, HEAD), bf16),
            pltpu.VMEM((STEPS, groups, half, HEAD), bf16),
            pltpu.VMEM((STEPS, groups, half, HEAD), bf16),
            pltpu.VMEM((heads, number, HEAD), f32),
            pltpu.VMEM((heads, number, HEAD), f32),
            pltpu.VMEM((heads, number, HEAD), f32),
            pltpu.VMEM((pairs, number, 2 * HEAD), bf16),
            pltpu.VMEM((pairs, number, 2 * HEAD), bf16),
            pltpu.VMEM((number, columns), f32),
            pltpu.SemaphoreType.DMA((10,)),
            pltpu.SemaphoreType.DMA((STEPS, groups + 1)),
            pltpu.SemaphoreType.DMA((STEPS, groups + 1)),
            pltpu.SemaphoreType.DMA((2, pairs)),
            pltpu.SemaphoreType.DMA((2, pairs)),
        ],
        compiler_params=pltpu.CompilerParams(collective_id=0, has_side_effects=True, vmem_limit_bytes=60 << 20),
    )(queries, keys, values, positions.reshape(number // HEAD, HEAD), frequency, out_weight)
    return pl.pallas_call(
        store,
        name="store",
        out_shape=jax.ShapeDtypeStruct((number, columns), bf16),
        in_specs=[pl.BlockSpec(memory_space=pltpu.MemorySpace.VMEM)],
        out_specs=pl.BlockSpec(memory_space=pltpu.MemorySpace.HBM),
        scratch_shapes=[pltpu.SemaphoreType.DMA((8,))],
    )(pltpu.with_memory_space_constraint(projected, pltpu.MemorySpace.VMEM))


def solution(mesh):
    in_specs = (P("ctx", "head"), P("ctx", "head"), P("ctx", "head"), P("ctx"), P(None, "head"))
    out_specs = P("ctx", "head")
    return jax.shard_map(shards, mesh=mesh, in_specs=in_specs, out_specs=out_specs, check_vma=False)
```

```python
import functools
import math

import jax
import jax.numpy as jnp
import numpy as np
from jax import lax
from jax.experimental import pallas as pl
from jax.experimental.pallas import tpu as pltpu
from jax.sharding import PartitionSpec as P

HEAD = 128
STEPS = 4
MASKED = -1e30
MESH = pl.DeviceIdType.MESH

PART_1 = 1.5703125
PART_2 = 507.0 / 2.0**20
PART_3 = math.pi / 2 - PART_1 - PART_2


def cosine_and_sine(angle, lane):
    turns = jnp.floor(angle * (2.0 / math.pi) + 0.5)
    rest = ((angle - turns * PART_1) - turns * PART_2) - turns * PART_3
    quadrant = turns.astype(jnp.int32) + jnp.where(lane < HEAD // 2, 1, 0)
    z = rest * rest
    sine = ((-1.9515295891e-4 * z + 8.3321608736e-3) * z - 1.6666654611e-1) * z * rest + rest
    cosine = ((2.443315711809948e-5 * z - 1.388731625493765e-3) * z + 4.166664568298827e-2) * z * z - 0.5 * z + 1.0
    value = jnp.where((quadrant & 1) == 1, cosine, sine)
    return jnp.where((quadrant & 2) == 2, -value, value)


def kernel(
    cycle,
    q_hbm, k_hbm, v_hbm, pos_hbm, freq_hbm, w_hbm,
    out_ref,
    q_in, k_in, v_in, pos_in, freq_in, weight,
    pos_col, cos_tab, sin_tab, q_rot, own_k, own_v, met_k, met_v, top, total, sums, att_own, att_met, mixed,
    load_sem, kv_send, kv_recv, x_send, x_recv, ready,
):
    block = lax.axis_index("ctx")
    head = lax.axis_index("head")
    half = q_in.shape[1] // 2
    pairs = q_in.shape[0]
    groups = own_k.shape[1]
    wide = 2 * HEAD
    scale = math.log2(math.e) / math.sqrt(HEAD)
    even = lax.rem(block, 2) == 0
    twin = jnp.where(even, block + 1, block - 1)

    small = [
        pltpu.make_async_copy(pos_hbm, pos_in, load_sem.at[0]),
        pltpu.make_async_copy(freq_hbm, freq_in, load_sem.at[1]),
        pltpu.make_async_copy(k_hbm, k_in, load_sem.at[2]),
        pltpu.make_async_copy(v_hbm, v_in, load_sem.at[3]),
    ]
    for copy in small:
        copy.start()
    q_loads = [
        pltpu.make_async_copy(q_hbm.at[:, pl.ds(p * wide, wide)], q_in.at[p], load_sem.at[4 + p]) for p in range(pairs)
    ]
    for copy in q_loads:
        copy.start()
    rows = weight.shape[1]
    w_loads = [
        pltpu.make_async_copy(w_hbm.at[pl.ds(pl.multiple_of(head * rows, rows), rows)], weight.at[0], load_sem.at[8]),
        pltpu.make_async_copy(
            w_hbm.at[pl.ds(pl.multiple_of((1 - head) * rows, rows), rows)], weight.at[1], load_sem.at[9]
        ),
    ]

    def at(step):
        return (lax.rem(block + step + cycle, cycle), head)

    place = lax.rem(block, 8)
    relay_one = place < 2
    relay_all = place == 3
    relay = relay_one | relay_all
    forth = jnp.where(relay_one, 8, 7)
    origin = jnp.where(place == 0, 7, jnp.where(place == 1, 5, 4))
    wrapped = relay & (block + forth >= cycle)
    fed_from = jnp.where(place == 2, -7, -8)
    fed = (place <= 2) & (block >= 8)

    def passes(step, piece):
        by_relay = (place == 7) if step == 3 else jnp.bool_(False)
        return by_relay | (place == 7) | ((place == 6) & (step == 3)) if piece >= 2 else by_relay

    def goal(step, piece):
        back = jnp.where((place == 7) & (step == 3), 7, 8)
        return at(jnp.where(passes(step, piece), step - back, step))

    barrier = pltpu.get_barrier_semaphore()

    def signal(semaphore, device):
        pl.semaphore_signal(semaphore, inc=1, device_id=device, device_id_type=MESH)

    for friend in (at(-1), (block, 1 - head), (twin, head)):
        signal(barrier, friend)
    pl.when(place != 2)(lambda: signal(barrier, at(-3)))
    pl.when((place <= 2) & (block < 8))(lambda: signal(barrier, at(fed_from)))

    @pl.when(relay)
    def _():
        signal(barrier, at(origin))
        pl.when(jnp.logical_not(wrapped))(lambda: signal(barrier, at(forth)))

    def enter():
        count = jnp.where(place >= 6, 5, 4) + jnp.where(fed, 1, 0) + jnp.where(wrapped, 1, 0)
        pl.semaphore_wait(barrier, count)
        pl.when(fed)(lambda: signal(ready, at(fed_from)))

    def own_piece(part, piece):
        return own_k.at[part, piece // 2] if piece % 2 else own_v.at[part, piece // 2]

    def met_piece(slot, piece):
        return met_k.at[slot, piece // 2] if piece % 2 else met_v.at[slot, piece // 2]

    def kv_copy(slot, step, piece):
        part = sent_part(step)
        there = jnp.where(passes(step, piece), STEPS - 1, step - 1)
        return pltpu.make_async_remote_copy(
            own_piece(part, piece), met_piece(there, piece), kv_send.at[slot, piece], kv_recv.at[there, piece],
            device_id=goal(step, piece), device_id_type=MESH,
        )

    def sent_part(step):
        return jnp.where(block + step < cycle, 0, 1)

    def keys_start(part):
        both = (sent_part(1) == part) & (sent_part(3) == part)

        @pl.when(both)
        def _():
            for piece in range(1, 2 * groups):
                kv_copy(0, 1, piece).start()
                kv_copy(1, 3, piece).start()

        for step in (1, 3):

            @pl.when((sent_part(step) == part) & jnp.logical_not(both))
            def _():
                for piece in range(1, 2 * groups):
                    kv_copy(step // 2, step, piece).start()

    first_step = jnp.where(even, 1, 3)
    other_step = 4 - first_step

    def hand_copy(piece):
        return pltpu.make_async_remote_copy(
            met_piece(first_step - 1, piece), met_piece(1, piece), kv_send.at[2, piece], kv_recv.at[1, piece],
            device_id=(twin, head), device_id_type=MESH,
        )

    def relay_copy(piece):
        there = jnp.where(place == 0, 0, 2)
        return pltpu.make_async_remote_copy(
            met_piece(STEPS - 1, piece), met_piece(there, piece), kv_send.at[3, piece], kv_recv.at[there, piece],
            device_id=at(forth), device_id_type=MESH,
        )

    def kv_wait(slot, piece):
        pltpu.make_async_remote_copy(
            met_piece(slot, piece), met_piece(slot, piece), kv_send.at[2, piece], kv_recv.at[slot, piece],
            device_id=(twin, head), device_id_type=MESH,
        ).wait_recv()

    for copy in small[3:]:
        copy.wait()
    for part in range(2):
        for group in range(groups):
            own_v[part, group] = v_in[pl.ds(part * half, half), pl.ds(group * HEAD, HEAD)]
    for copy in small[:3]:
        copy.wait()
    lane = lax.broadcasted_iota(jnp.int32, (HEAD, HEAD), 1)
    frequency = freq_in[0:1, :]

    def rotated(block_rows, cut):
        value = block_rows.astype(jnp.float32)
        return (value * cos_tab[cut, :] + pltpu.roll(value, HEAD // 2, 1) * sin_tab[cut, :]).astype(jnp.bfloat16)

    def prepare(part):
        for i in range(half // HEAD):
            cut = pl.ds(pl.multiple_of(part * half + i * HEAD, HEAD), HEAD)
            line = pos_in[pl.ds(part * (half // HEAD) + i, 1), :].astype(jnp.float32)
            column = jnp.transpose(jnp.broadcast_to(line, (HEAD, HEAD)))
            pos_col[cut, :] = column.astype(jnp.int32)
            both = cosine_and_sine(column * frequency, lane)
            other = pltpu.roll(both, HEAD // 2, 1)
            cos_tab[cut, :] = jnp.where(lane < HEAD // 2, both, other)
            sin_tab[cut, :] = jnp.where(lane < HEAD // 2, -other, both)
        cut = pl.ds(pl.multiple_of(part * half, half), half)
        for group in range(groups):
            own_k[part, group] = rotated(k_in[cut, pl.ds(group * HEAD, HEAD)], cut)

    def x_copy(part, order, p):
        cut = pl.ds(pl.multiple_of(part * half, half), half)
        return pltpu.make_async_remote_copy(
            att_own.at[p, cut], att_met.at[p, cut], x_send.at[order, p], x_recv.at[order, p],
            device_id=(block, 1 - head), device_id_type=MESH,
        )

    far = block < STEPS - 1

    first = jnp.where(far, 0, 1)
    second = 1 - first
    alone = jnp.logical_not(far) | (block == 0)

    row_at = lax.broadcasted_iota(jnp.int32, (half, wide), 0)
    key_at = lax.broadcasted_iota(jnp.int32, (half, wide), 1)
    per_group = pairs // groups

    def both_lanes(value):
        return jnp.concatenate([value, value], axis=1)

    def finish(part, p):
        cut = pl.ds(pl.multiple_of(part * half, half), half)
        for n in range(2):
            share = 1.0 / jnp.sum(total[2 * p + n, cut, :], axis=1, keepdims=True)
            att_own[p, cut, n * HEAD : (n + 1) * HEAD] = (sums[2 * p + n, cut, :] * share).astype(jnp.bfloat16)

    def own_block(part, p):
        cut = pl.ds(pl.multiple_of(part * half, half), half)
        group = p // per_group
        keys = own_k[part, group]
        values = own_v[part, group]
        reach = both_lanes(pos_col[cut, :])
        seen = (key_at <= row_at) & (key_at >= row_at - reach)
        for m in range(2):
            lanes = slice(m * HEAD, (m + 1) * HEAD)
            h = 2 * p + m
            query = rotated(q_in[p, cut, lanes], cut)
            q_rot[p, cut, lanes] = query
            scores = lax.dot_general(query, keys, (((1,), (1,)), ((), ())), preferred_element_type=jnp.float32)
            scores = jnp.where(seen, scores, MASKED)
            highest = jnp.broadcast_to(jnp.max(scores, axis=1, keepdims=True), (half, HEAD))
            weights = jnp.exp2((scores - both_lanes(highest)) * scale)
            top[h, cut, :] = highest
            total[h, cut, :] = weights[:, :HEAD] + weights[:, HEAD:]
            sums[h, cut, :] = jnp.dot(weights.astype(jnp.bfloat16), values, preferred_element_type=jnp.float32)

    def pass_on(piece):
        kv_wait(STEPS - 1, piece)
        relay_copy(piece).start()

    def first_own(p, carry):
        own_block(first, p)

        @pl.when(alone)
        def _():
            finish(first, p)
            x_copy(first, 0, p).start()

        @pl.when(p == 0)
        def _():
            prepare(second)
            keys_start(second)

        @pl.when(relay_all & (p == pairs - 2))
        def _():
            pl.when(jnp.logical_not(wrapped))(lambda: pl.semaphore_wait(ready, 1))
            pass_on(0)

        return carry

    def second_own(group, carry):
        for m in range(per_group):
            own_block(second, group * per_group + m)

        @pl.when(relay & (group == 0))
        def _():
            pl.when(relay_all)(lambda: pass_on(1))
            pl.when(relay_one & jnp.logical_not(wrapped))(lambda: pl.semaphore_wait(ready, 1))
            for piece in range(2, 2 * groups):
                pass_on(piece)

        return carry

    prepare(first)
    enter()
    kv_copy(0, 1, 0).start()
    kv_copy(1, 3, 0).start()
    keys_start(first)
    for copy in q_loads:
        copy.wait()
    for copy in w_loads:
        copy.start()
    lax.fori_loop(0, pairs, first_own, 0)
    lax.fori_loop(0, groups, second_own, 0)

    def met_block(step, group):
        early = step <= block
        part = jnp.where(early, 0, 1)
        apart = jnp.where(early, step, cycle - step) * half
        cut = pl.ds(pl.multiple_of(part * half, half), half)
        keys = met_k[step - 1, group]
        values = met_v[step - 1, group]
        reach = both_lanes(pos_col[cut, :])
        seen = key_at >= row_at - reach + apart
        for m in range(2 * per_group):
            p = group * per_group + m // 2
            lanes = slice((m % 2) * HEAD, (m % 2 + 1) * HEAD)
            h = 2 * group * per_group + m
            query = q_rot[p, cut, lanes]
            scores = lax.dot_general(query, keys, (((1,), (1,)), ((), ())), preferred_element_type=jnp.float32)
            scores = jnp.where(seen, scores, MASKED)
            before = top[h, cut, :]
            highest = jnp.maximum(before, jnp.max(scores, axis=1, keepdims=True))
            factor = jnp.exp2((before - highest) * scale)
            weights = jnp.exp2((scores - both_lanes(highest)) * scale)
            top[h, cut, :] = highest
            total[h, cut, :] = total[h, cut, :] * factor + (weights[:, :HEAD] + weights[:, HEAD:])
            sums[h, cut, :] = sums[h, cut, :] * factor + jnp.dot(
                weights.astype(jnp.bfloat16), values, preferred_element_type=jnp.float32
            )
        return part

    def pick(i, usual, one, two):
        def listed(values):
            value = jnp.int32(values[-1])
            for n in range(len(values) - 1):
                value = jnp.where(i == n, values[n], value)
            return value

        return jnp.where(block == 1, listed(one), jnp.where(block == 2, listed(two), listed(usual)))

    def usual_steps(group):
        late = (place < 2) & (group == 1)
        return (
            jnp.where(late, other_step, first_step),
            jnp.where(late, first_step, jnp.where(place == 2, 2, other_step)),
            jnp.where(place == 2, other_step, 2),
        )

    def meeting(i, carry):
        group = pick(i, (0, 0, 0, 1, 1, 1), (0, 1, 0, 0, 1, 1), (0, 0, 1, 1, 0, 1))
        turn = pick(i, (-1, -2, -3, -1, -2, -3), (1, 1, 3, 2, 3, 2), (1, 2, 1, 2, 3, 3))
        step = turn
        for n in range(STEPS - 1):
            step = jnp.where(turn == -1 - n, usual_steps(group)[n], step)
        done = pick(i, (0, 0, 1, 0, 0, 1), (1, 1, 0, 1, 0, 1), (0, 1, 0, 1, 1, 1))
        handing = step == first_step

        def arrive(known):
            for piece in (2 * known, 2 * known + 1):
                kv_wait(step - 1, piece)
                pl.when(handing)(lambda: hand_copy(piece).start())

        for known in range(groups):
            pl.when(group == known)(lambda: arrive(known))
        part = met_block(step, group)

        @pl.when(done == 1)
        def _():
            for m in range(per_group):
                p = group * per_group + m
                finish(part, p)
                x_copy(part, jnp.where(part == first, 0, 1), p).start()

        return carry

    lax.fori_loop(0, 2 * (STEPS - 1), meeting, 0)

    tile = 256
    tiles = out_ref.shape[1] // tile

    def project(part, own, met, fresh, last):
        cut = pl.ds(pl.multiple_of(part * half, half), half)

        for t in range(tiles):
            columns = slice(t * tile, (t + 1) * tile)
            value = None if fresh else mixed[cut, columns]
            for which, att, (begin, end) in ((0, att_own, own), (1, att_met, met)):
                if begin < end:
                    left = jnp.concatenate([att[p, cut, :] for p in range(begin, end)], axis=1)
                    right = weight[which, begin * wide : end * wide, columns]
                    more = jnp.dot(left, right, preferred_element_type=jnp.float32)
                    value = more if value is None else value + more
            if last:
                out_ref[cut, columns] = value.astype(jnp.bfloat16)
            else:
                mixed[cut, columns] = value

    for copy in w_loads:
        copy.wait()
    for p in range(pairs):
        x_copy(first, 0, p).wait_recv()
    project(first, (0, pairs), (0, pairs), True, True)
    for p in range(per_group):
        x_copy(second, 1, p).wait_recv()
    project(second, (0, pairs), (0, per_group), True, False)
    for p in range(per_group, pairs):
        x_copy(second, 1, p).wait_recv()
        project(second, (0, 0), (p, p + 1), False, p == pairs - 1)

    for p in range(pairs):
        x_copy(first, 0, p).wait_send()
        x_copy(second, 1, p).wait_send()
    for piece in range(2 * groups):
        kv_copy(0, 1, piece).wait_send()
        kv_copy(1, 3, piece).wait_send()
        hand_copy(piece).wait_send()

    @pl.when(relay)
    def _():
        for piece in range(2, 2 * groups):
            relay_copy(piece).wait_send()

    @pl.when(relay_all)
    def _():
        for piece in range(2):
            relay_copy(piece).wait_send()


def store(value_ref, out_hbm, sem):
    rows = value_ref.shape[0] // sem.shape[0]
    copies = [
        pltpu.make_async_copy(value_ref.at[pl.ds(i * rows, rows)], out_hbm.at[pl.ds(i * rows, rows)], sem.at[i])
        for i in range(sem.shape[0])
    ]
    for copy in copies:
        copy.start()
    for copy in copies:
        copy.wait()


def shards(queries, keys, values, positions, out_weight):
    number, width = queries.shape
    half = number // 2
    pairs = width // (2 * HEAD)
    groups = keys.shape[1] // HEAD
    heads = width // HEAD
    columns = out_weight.shape[1]
    cycle = lax.axis_size("ctx")
    table = np.power(500000.0, -2.0 * np.arange(HEAD // 2) / HEAD).astype(np.float32)
    frequency = jnp.asarray(np.tile(np.concatenate([table, table])[None, :], (8, 1)))
    f32, bf16, i32 = jnp.float32, jnp.bfloat16, jnp.int32
    hbm = pl.BlockSpec(memory_space=pltpu.MemorySpace.HBM)
    projected = pl.pallas_call(
        functools.partial(kernel, cycle),
        name="attend_and_project",
        out_shape=pltpu.VMEM((number, columns), bf16),
        in_specs=[hbm] * 6,
        out_specs=pl.BlockSpec(memory_space=pltpu.MemorySpace.VMEM),
        scratch_shapes=[
            pltpu.VMEM((pairs, number, 2 * HEAD), bf16),
            pltpu.VMEM((number, groups * HEAD), bf16),
            pltpu.VMEM((number, groups * HEAD), bf16),
            pltpu.VMEM((number // HEAD, HEAD), i32),
            pltpu.VMEM((8, HEAD), f32),
            pltpu.VMEM((2, width, columns), bf16),
            pltpu.VMEM((number, HEAD), i32),
            pltpu.VMEM((number, HEAD), f32),
            pltpu.VMEM((number, HEAD), f32),
            pltpu.VMEM((pairs, number, 2 * HEAD), bf16),
            pltpu.VMEM((2, groups, half, HEAD), bf16),
            pltpu.VMEM((2, groups, half, HEAD), bf16),
            pltpu.VMEM((STEPS, groups, half, HEAD), bf16),
            pltpu.VMEM((STEPS, groups, half, HEAD), bf16),
            pltpu.VMEM((heads, number, HEAD), f32),
            pltpu.VMEM((heads, number, HEAD), f32),
            pltpu.VMEM((heads, number, HEAD), f32),
            pltpu.VMEM((pairs, number, 2 * HEAD), bf16),
            pltpu.VMEM((pairs, number, 2 * HEAD), bf16),
            pltpu.VMEM((number, columns), f32),
            pltpu.SemaphoreType.DMA((10,)),
            pltpu.SemaphoreType.DMA((STEPS, 2 * groups)),
            pltpu.SemaphoreType.DMA((STEPS, 2 * groups)),
            pltpu.SemaphoreType.DMA((2, pairs)),
            pltpu.SemaphoreType.DMA((2, pairs)),
            pltpu.SemaphoreType.REGULAR,
        ],
        compiler_params=pltpu.CompilerParams(collective_id=0, has_side_effects=True, vmem_limit_bytes=60 << 20),
    )(queries, keys, values, positions.reshape(number // HEAD, HEAD), frequency, out_weight)
    return pl.pallas_call(
        store,
        name="store",
        out_shape=jax.ShapeDtypeStruct((number, columns), bf16),
        in_specs=[pl.BlockSpec(memory_space=pltpu.MemorySpace.VMEM)],
        out_specs=pl.BlockSpec(memory_space=pltpu.MemorySpace.HBM),
        scratch_shapes=[pltpu.SemaphoreType.DMA((4,))],
    )(pltpu.with_memory_space_constraint(projected, pltpu.MemorySpace.VMEM))


def solution(mesh):
    in_specs = (P("ctx", "head"), P("ctx", "head"), P("ctx", "head"), P("ctx"), P(None, "head"))
    out_specs = P("ctx", "head")
    return jax.shard_map(shards, mesh=mesh, in_specs=in_specs, out_specs=out_specs, check_vma=False)
```

```python
import functools
import math

import jax
import jax.numpy as jnp
import numpy as np
from jax import lax
from jax.experimental import pallas as pl
from jax.experimental.pallas import tpu as pltpu
from jax.sharding import PartitionSpec as P

HEAD = 128
STEPS = 4
MASKED = -1e30
MESH = pl.DeviceIdType.MESH

PART_1 = 1.5703125
PART_2 = 507.0 / 2.0**20
PART_3 = math.pi / 2 - PART_1 - PART_2


def cosine_and_sine(angle, lane):
    turns = jnp.floor(angle * (2.0 / math.pi) + 0.5)
    rest = ((angle - turns * PART_1) - turns * PART_2) - turns * PART_3
    quadrant = turns.astype(jnp.int32) + jnp.where(lane < HEAD // 2, 1, 0)
    z = rest * rest
    sine = ((-1.9515295891e-4 * z + 8.3321608736e-3) * z - 1.6666654611e-1) * z * rest + rest
    cosine = ((2.443315711809948e-5 * z - 1.388731625493765e-3) * z + 4.166664568298827e-2) * z * z - 0.5 * z + 1.0
    value = jnp.where((quadrant & 1) == 1, cosine, sine)
    return jnp.where((quadrant & 2) == 2, -value, value)


def kernel(
    cycle,
    q_hbm, k_hbm, v_hbm, pos_hbm, freq_hbm, w_hbm,
    out_ref,
    q_in, k_in, v_in, pos_in, freq_in, weight,
    pos_col, cos_tab, sin_tab, q_rot, own_k, own_v, met_k, met_v, top, total, sums, att_own, att_met, mixed,
    load_sem, kv_send, kv_recv, x_send, x_recv, ready,
):
    block = lax.axis_index("ctx")
    head = lax.axis_index("head")
    half = q_in.shape[1] // 2
    pairs = q_in.shape[0]
    groups = own_k.shape[1]
    wide = 2 * HEAD
    scale = math.log2(math.e) / math.sqrt(HEAD)
    even = lax.rem(block, 2) == 0
    twin = jnp.where(even, block + 1, block - 1)

    small = [
        pltpu.make_async_copy(pos_hbm, pos_in, load_sem.at[0]),
        pltpu.make_async_copy(freq_hbm, freq_in, load_sem.at[1]),
        pltpu.make_async_copy(k_hbm, k_in, load_sem.at[2]),
        pltpu.make_async_copy(v_hbm, v_in, load_sem.at[3]),
    ]
    for copy in small:
        copy.start()
    q_loads = [
        pltpu.make_async_copy(q_hbm.at[:, pl.ds(p * wide, wide)], q_in.at[p], load_sem.at[4 + p]) for p in range(pairs)
    ]
    for copy in q_loads:
        copy.start()
    rows = weight.shape[1]
    w_loads = [
        pltpu.make_async_copy(w_hbm.at[pl.ds(pl.multiple_of(head * rows, rows), rows)], weight.at[0], load_sem.at[8]),
        pltpu.make_async_copy(
            w_hbm.at[pl.ds(pl.multiple_of((1 - head) * rows, rows), rows)], weight.at[1], load_sem.at[9]
        ),
    ]

    def at(step):
        return (lax.rem(block + step + cycle, cycle), head)

    place = lax.rem(block, 8)
    relay_one = place < 2
    relay_all = place == 3
    relay = relay_one | relay_all
    forth = jnp.where(relay_one, 8, 7)
    origin = jnp.where(place == 0, 7, jnp.where(place == 1, 5, 4))
    wrapped = relay & (block + forth >= cycle)
    fed_from = jnp.where(place == 2, -7, -8)
    fed = (place <= 2) & (block >= 8)

    def passes(step, piece):
        by_relay = (place == 7) if step == 3 else jnp.bool_(False)
        return by_relay | (place == 7) | ((place == 6) & (step == 3)) if piece >= 2 else by_relay

    def goal(step, piece):
        back = jnp.where((place == 7) & (step == 3), 7, 8)
        return at(jnp.where(passes(step, piece), step - back, step))

    barrier = pltpu.get_barrier_semaphore()

    def signal(semaphore, device):
        pl.semaphore_signal(semaphore, inc=1, device_id=device, device_id_type=MESH)

    for friend in (at(-1), (block, 1 - head), (twin, head)):
        signal(barrier, friend)
    pl.when(place != 2)(lambda: signal(barrier, at(-3)))
    pl.when((place <= 2) & (block < 8))(lambda: signal(barrier, at(fed_from)))

    @pl.when(relay)
    def _():
        signal(barrier, at(origin))
        pl.when(jnp.logical_not(wrapped))(lambda: signal(barrier, at(forth)))

    def enter():
        count = jnp.where(place >= 6, 5, 4) + jnp.where(fed, 1, 0) + jnp.where(wrapped, 1, 0)
        pl.semaphore_wait(barrier, count)
        pl.when(fed)(lambda: signal(ready, at(fed_from)))

    def own_piece(part, piece):
        return own_k.at[part, piece // 2] if piece % 2 else own_v.at[part, piece // 2]

    def met_piece(slot, piece):
        return met_k.at[slot, piece // 2] if piece % 2 else met_v.at[slot, piece // 2]

    def kv_copy(slot, step, piece):
        part = sent_part(step)
        there = jnp.where(passes(step, piece), STEPS - 1, step - 1)
        return pltpu.make_async_remote_copy(
            own_piece(part, piece), met_piece(there, piece), kv_send.at[slot, piece], kv_recv.at[there, piece],
            device_id=goal(step, piece), device_id_type=MESH,
        )

    def sent_part(step):
        return jnp.where(block + step < cycle, 0, 1)

    def keys_start(part):
        both = (sent_part(1) == part) & (sent_part(3) == part)

        @pl.when(both)
        def _():
            for piece in range(1, 2 * groups):
                kv_copy(0, 1, piece).start()
                kv_copy(1, 3, piece).start()

        for step in (1, 3):

            @pl.when((sent_part(step) == part) & jnp.logical_not(both))
            def _():
                for piece in range(1, 2 * groups):
                    kv_copy(step // 2, step, piece).start()

    first_step = jnp.where(even, 1, 3)
    other_step = 4 - first_step

    def hand_copy(piece):
        return pltpu.make_async_remote_copy(
            met_piece(first_step - 1, piece), met_piece(1, piece), kv_send.at[2, piece], kv_recv.at[1, piece],
            device_id=(twin, head), device_id_type=MESH,
        )

    def relay_copy(piece):
        there = jnp.where(place == 0, 0, 2)
        return pltpu.make_async_remote_copy(
            met_piece(STEPS - 1, piece), met_piece(there, piece), kv_send.at[3, piece], kv_recv.at[there, piece],
            device_id=at(forth), device_id_type=MESH,
        )

    def kv_wait(slot, piece):
        pltpu.make_async_remote_copy(
            met_piece(slot, piece), met_piece(slot, piece), kv_send.at[2, piece], kv_recv.at[slot, piece],
            device_id=(twin, head), device_id_type=MESH,
        ).wait_recv()

    for copy in small[3:]:
        copy.wait()
    for part in range(2):
        for group in range(groups):
            own_v[part, group] = v_in[pl.ds(part * half, half), pl.ds(group * HEAD, HEAD)]
    for copy in small[:3]:
        copy.wait()
    lane = lax.broadcasted_iota(jnp.int32, (HEAD, HEAD), 1)
    frequency = freq_in[0:1, :]

    def rotated(block_rows, cut):
        value = block_rows.astype(jnp.float32)
        return (value * cos_tab[cut, :] + pltpu.roll(value, HEAD // 2, 1) * sin_tab[cut, :]).astype(jnp.bfloat16)

    def prepare(part):
        for i in range(half // HEAD):
            cut = pl.ds(pl.multiple_of(part * half + i * HEAD, HEAD), HEAD)
            line = pos_in[pl.ds(part * (half // HEAD) + i, 1), :].astype(jnp.float32)
            column = jnp.transpose(jnp.broadcast_to(line, (HEAD, HEAD)))
            pos_col[cut, :] = column.astype(jnp.int32)
            both = cosine_and_sine(column * frequency, lane)
            other = pltpu.roll(both, HEAD // 2, 1)
            cos_tab[cut, :] = jnp.where(lane < HEAD // 2, both, other)
            sin_tab[cut, :] = jnp.where(lane < HEAD // 2, -other, both)
        cut = pl.ds(pl.multiple_of(part * half, half), half)
        for group in range(groups):
            own_k[part, group] = rotated(k_in[cut, pl.ds(group * HEAD, HEAD)], cut)

    def x_copy(part, order, p):
        cut = pl.ds(pl.multiple_of(part * half, half), half)
        return pltpu.make_async_remote_copy(
            att_own.at[p, cut], att_met.at[p, cut], x_send.at[order, p], x_recv.at[order, p],
            device_id=(block, 1 - head), device_id_type=MESH,
        )

    far = block < STEPS - 1

    first = jnp.where(far, 0, 1)
    second = 1 - first
    alone = jnp.logical_not(far) | (block == 0)

    row_at = lax.broadcasted_iota(jnp.int32, (half, wide), 0)
    key_at = lax.broadcasted_iota(jnp.int32, (half, wide), 1)
    per_group = pairs // groups

    def both_lanes(value):
        return jnp.concatenate([value, value], axis=1)

    def finish(part, p):
        cut = pl.ds(pl.multiple_of(part * half, half), half)
        for n in range(2):
            share = 1.0 / jnp.sum(total[2 * p + n, cut, :], axis=1, keepdims=True)
            att_own[p, cut, n * HEAD : (n + 1) * HEAD] = (sums[2 * p + n, cut, :] * share).astype(jnp.bfloat16)

    def own_block(part, p):
        cut = pl.ds(pl.multiple_of(part * half, half), half)
        group = p // per_group
        keys = own_k[part, group]
        values = own_v[part, group]
        reach = both_lanes(pos_col[cut, :])
        seen = (key_at <= row_at) & (key_at >= row_at - reach)
        for m in range(2):
            lanes = slice(m * HEAD, (m + 1) * HEAD)
            h = 2 * p + m
            query = rotated(q_in[p, cut, lanes], cut)
            q_rot[p, cut, lanes] = query
            scores = lax.dot_general(query, keys, (((1,), (1,)), ((), ())), preferred_element_type=jnp.float32)
            scores = jnp.where(seen, scores, MASKED)
            highest = jnp.broadcast_to(jnp.max(scores, axis=1, keepdims=True), (half, HEAD))
            weights = jnp.exp2((scores - both_lanes(highest)) * scale)
            top[h, cut, :] = highest
            total[h, cut, :] = weights[:, :HEAD] + weights[:, HEAD:]
            sums[h, cut, :] = jnp.dot(weights.astype(jnp.bfloat16), values, preferred_element_type=jnp.float32)

    def pass_on(piece):
        kv_wait(STEPS - 1, piece)
        relay_copy(piece).start()

    def first_own(p, carry):
        own_block(first, p)

        @pl.when(alone)
        def _():
            finish(first, p)
            x_copy(first, 0, p).start()

        @pl.when(p == 0)
        def _():
            prepare(second)
            keys_start(second)

        @pl.when(relay_all & (p == pairs - 2))
        def _():
            pl.when(jnp.logical_not(wrapped))(lambda: pl.semaphore_wait(ready, 1))
            pass_on(0)

        return carry

    def second_own(group, carry):
        for m in range(per_group):
            own_block(second, group * per_group + m)

        @pl.when((relay_all & (group == 0)) | (relay_one & (group == 1)))
        def _():
            pl.when(relay_all)(lambda: pass_on(1))
            pl.when(relay_one & jnp.logical_not(wrapped))(lambda: pl.semaphore_wait(ready, 1))
            for piece in range(2, 2 * groups):
                pass_on(piece)

        return carry

    prepare(first)
    enter()
    kv_copy(0, 1, 0).start()
    kv_copy(1, 3, 0).start()
    keys_start(first)
    for copy in q_loads:
        copy.wait()
    for copy in w_loads:
        copy.start()
    lax.fori_loop(0, pairs, first_own, 0)
    lax.fori_loop(0, groups, second_own, 0)

    def met_block(step, group):
        early = step <= block
        part = jnp.where(early, 0, 1)
        apart = jnp.where(early, step, cycle - step) * half
        cut = pl.ds(pl.multiple_of(part * half, half), half)
        keys = met_k[step - 1, group]
        values = met_v[step - 1, group]
        reach = both_lanes(pos_col[cut, :])
        seen = key_at >= row_at - reach + apart
        for m in range(2 * per_group):
            p = group * per_group + m // 2
            lanes = slice((m % 2) * HEAD, (m % 2 + 1) * HEAD)
            h = 2 * group * per_group + m
            query = q_rot[p, cut, lanes]
            scores = lax.dot_general(query, keys, (((1,), (1,)), ((), ())), preferred_element_type=jnp.float32)
            scores = jnp.where(seen, scores, MASKED)
            before = top[h, cut, :]
            highest = jnp.maximum(before, jnp.max(scores, axis=1, keepdims=True))
            factor = jnp.exp2((before - highest) * scale)
            weights = jnp.exp2((scores - both_lanes(highest)) * scale)
            top[h, cut, :] = highest
            total[h, cut, :] = total[h, cut, :] * factor + (weights[:, :HEAD] + weights[:, HEAD:])
            sums[h, cut, :] = sums[h, cut, :] * factor + jnp.dot(
                weights.astype(jnp.bfloat16), values, preferred_element_type=jnp.float32
            )
        return part

    def pick(i, usual, one, two):
        def listed(values):
            value = jnp.int32(values[-1])
            for n in range(len(values) - 1):
                value = jnp.where(i == n, values[n], value)
            return value

        return jnp.where(block == 1, listed(one), jnp.where(block == 2, listed(two), listed(usual)))

    def usual_steps(group):
        late = (place < 2) & (group == 1)
        return (
            jnp.where(late, other_step, first_step),
            jnp.where(late, first_step, jnp.where(place == 2, 2, other_step)),
            jnp.where(place == 2, other_step, 2),
        )

    def meeting(i, carry):
        group = pick(i, (0, 0, 0, 1, 1, 1), (0, 1, 0, 0, 1, 1), (0, 0, 1, 1, 0, 1))
        turn = pick(i, (-1, -2, -3, -1, -2, -3), (1, 1, 3, 2, 3, 2), (1, 2, 1, 2, 3, 3))
        step = turn
        for n in range(STEPS - 1):
            step = jnp.where(turn == -1 - n, usual_steps(group)[n], step)
        done = pick(i, (0, 0, 1, 0, 0, 1), (1, 1, 0, 1, 0, 1), (0, 1, 0, 1, 1, 1))
        handing = step == first_step

        def arrive(known):
            for piece in (2 * known, 2 * known + 1):
                kv_wait(step - 1, piece)
                pl.when(handing)(lambda: hand_copy(piece).start())

        for known in range(groups):
            pl.when(group == known)(lambda: arrive(known))
        part = met_block(step, group)

        @pl.when(done == 1)
        def _():
            for m in range(per_group):
                p = group * per_group + m
                finish(part, p)
                x_copy(part, jnp.where(part == first, 0, 1), p).start()

        return carry

    lax.fori_loop(0, 2 * (STEPS - 1), meeting, 0)

    tile = 256
    tiles = out_ref.shape[1] // tile

    def project(part, own, met, fresh, last):
        cut = pl.ds(pl.multiple_of(part * half, half), half)

        for t in range(tiles):
            columns = slice(t * tile, (t + 1) * tile)
            value = None if fresh else mixed[cut, columns]
            for which, att, (begin, end) in ((0, att_own, own), (1, att_met, met)):
                if begin < end:
                    left = jnp.concatenate([att[p, cut, :] for p in range(begin, end)], axis=1)
                    right = weight[which, begin * wide : end * wide, columns]
                    more = jnp.dot(left, right, preferred_element_type=jnp.float32)
                    value = more if value is None else value + more
            if last:
                out_ref[cut, columns] = value.astype(jnp.bfloat16)
            else:
                mixed[cut, columns] = value

    for copy in w_loads:
        copy.wait()
    for p in range(pairs):
        x_copy(first, 0, p).wait_recv()
    project(first, (0, pairs), (0, pairs), True, True)
    for p in range(per_group):
        x_copy(second, 1, p).wait_recv()
    project(second, (0, pairs), (0, per_group), True, False)
    for p in range(per_group, pairs):
        x_copy(second, 1, p).wait_recv()
        project(second, (0, 0), (p, p + 1), False, p == pairs - 1)

    for p in range(pairs):
        x_copy(first, 0, p).wait_send()
        x_copy(second, 1, p).wait_send()
    for piece in range(2 * groups):
        kv_copy(0, 1, piece).wait_send()
        kv_copy(1, 3, piece).wait_send()
        hand_copy(piece).wait_send()

    @pl.when(relay)
    def _():
        for piece in range(2, 2 * groups):
            relay_copy(piece).wait_send()

    @pl.when(relay_all)
    def _():
        for piece in range(2):
            relay_copy(piece).wait_send()


def store(value_ref, out_hbm, sem):
    rows = value_ref.shape[0] // sem.shape[0]
    copies = [
        pltpu.make_async_copy(value_ref.at[pl.ds(i * rows, rows)], out_hbm.at[pl.ds(i * rows, rows)], sem.at[i])
        for i in range(sem.shape[0])
    ]
    for copy in copies:
        copy.start()
    for copy in copies:
        copy.wait()


def shards(queries, keys, values, positions, out_weight):
    number, width = queries.shape
    half = number // 2
    pairs = width // (2 * HEAD)
    groups = keys.shape[1] // HEAD
    heads = width // HEAD
    columns = out_weight.shape[1]
    cycle = lax.axis_size("ctx")
    table = np.power(500000.0, -2.0 * np.arange(HEAD // 2) / HEAD).astype(np.float32)
    frequency = jnp.asarray(np.tile(np.concatenate([table, table])[None, :], (8, 1)))
    f32, bf16, i32 = jnp.float32, jnp.bfloat16, jnp.int32
    hbm = pl.BlockSpec(memory_space=pltpu.MemorySpace.HBM)
    projected = pl.pallas_call(
        functools.partial(kernel, cycle),
        name="attend_and_project",
        out_shape=pltpu.VMEM((number, columns), bf16),
        in_specs=[hbm] * 6,
        out_specs=pl.BlockSpec(memory_space=pltpu.MemorySpace.VMEM),
        scratch_shapes=[
            pltpu.VMEM((pairs, number, 2 * HEAD), bf16),
            pltpu.VMEM((number, groups * HEAD), bf16),
            pltpu.VMEM((number, groups * HEAD), bf16),
            pltpu.VMEM((number // HEAD, HEAD), i32),
            pltpu.VMEM((8, HEAD), f32),
            pltpu.VMEM((2, width, columns), bf16),
            pltpu.VMEM((number, HEAD), i32),
            pltpu.VMEM((number, HEAD), f32),
            pltpu.VMEM((number, HEAD), f32),
            pltpu.VMEM((pairs, number, 2 * HEAD), bf16),
            pltpu.VMEM((2, groups, half, HEAD), bf16),
            pltpu.VMEM((2, groups, half, HEAD), bf16),
            pltpu.VMEM((STEPS, groups, half, HEAD), bf16),
            pltpu.VMEM((STEPS, groups, half, HEAD), bf16),
            pltpu.VMEM((heads, number, HEAD), f32),
            pltpu.VMEM((heads, number, HEAD), f32),
            pltpu.VMEM((heads, number, HEAD), f32),
            pltpu.VMEM((pairs, number, 2 * HEAD), bf16),
            pltpu.VMEM((pairs, number, 2 * HEAD), bf16),
            pltpu.VMEM((number, columns), f32),
            pltpu.SemaphoreType.DMA((10,)),
            pltpu.SemaphoreType.DMA((STEPS, 2 * groups)),
            pltpu.SemaphoreType.DMA((STEPS, 2 * groups)),
            pltpu.SemaphoreType.DMA((2, pairs)),
            pltpu.SemaphoreType.DMA((2, pairs)),
            pltpu.SemaphoreType.REGULAR,
        ],
        compiler_params=pltpu.CompilerParams(collective_id=0, has_side_effects=True, vmem_limit_bytes=60 << 20),
    )(queries, keys, values, positions.reshape(number // HEAD, HEAD), frequency, out_weight)
    return pl.pallas_call(
        store,
        name="store",
        out_shape=jax.ShapeDtypeStruct((number, columns), bf16),
        in_specs=[pl.BlockSpec(memory_space=pltpu.MemorySpace.VMEM)],
        out_specs=pl.BlockSpec(memory_space=pltpu.MemorySpace.HBM),
        scratch_shapes=[pltpu.SemaphoreType.DMA((4,))],
    )(pltpu.with_memory_space_constraint(projected, pltpu.MemorySpace.VMEM))


def solution(mesh):
    in_specs = (P("ctx", "head"), P("ctx", "head"), P("ctx", "head"), P("ctx"), P(None, "head"))
    out_specs = P("ctx", "head")
    return jax.shard_map(shards, mesh=mesh, in_specs=in_specs, out_specs=out_specs, check_vma=False)
```

```python
import functools
import math

import jax
import jax.numpy as jnp
import numpy as np
from jax import lax
from jax.experimental import pallas as pl
from jax.experimental.pallas import tpu as pltpu
from jax.sharding import PartitionSpec as P

HEAD = 128
STEPS = 4
MASKED = -1e30
MESH = pl.DeviceIdType.MESH

PART_1 = 1.5703125
PART_2 = 507.0 / 2.0**20
PART_3 = math.pi / 2 - PART_1 - PART_2


def cosine_and_sine(angle, lane):
    turns = jnp.floor(angle * (2.0 / math.pi) + 0.5)
    rest = ((angle - turns * PART_1) - turns * PART_2) - turns * PART_3
    quadrant = turns.astype(jnp.int32) + jnp.where(lane < HEAD // 2, 1, 0)
    z = rest * rest
    sine = ((-1.9515295891e-4 * z + 8.3321608736e-3) * z - 1.6666654611e-1) * z * rest + rest
    cosine = ((2.443315711809948e-5 * z - 1.388731625493765e-3) * z + 4.166664568298827e-2) * z * z - 0.5 * z + 1.0
    value = jnp.where((quadrant & 1) == 1, cosine, sine)
    return jnp.where((quadrant & 2) == 2, -value, value)


def kernel(
    cycle,
    q_hbm, k_hbm, v_hbm, pos_hbm, freq_hbm, w_hbm,
    out_ref,
    q_in, k_in, v_in, pos_in, freq_in, weight,
    pos_col, cos_tab, sin_tab, q_rot, own_k, own_v, met_k, met_v, top, total, sums, att_own, att_met, mixed,
    load_sem, kv_send, kv_recv, x_send, x_recv, ready,
):
    block = lax.axis_index("ctx")
    head = lax.axis_index("head")
    half = q_in.shape[1] // 2
    pairs = q_in.shape[0]
    groups = own_k.shape[1]
    wide = 2 * HEAD
    scale = math.log2(math.e) / math.sqrt(HEAD)
    even = lax.rem(block, 2) == 0
    twin = jnp.where(even, block + 1, block - 1)

    small = [
        pltpu.make_async_copy(pos_hbm, pos_in, load_sem.at[0]),
        pltpu.make_async_copy(freq_hbm, freq_in, load_sem.at[1]),
        pltpu.make_async_copy(k_hbm, k_in, load_sem.at[2]),
        pltpu.make_async_copy(v_hbm, v_in, load_sem.at[3]),
    ]
    for copy in small:
        copy.start()
    q_loads = [
        pltpu.make_async_copy(q_hbm.at[:, pl.ds(p * wide, wide)], q_in.at[p], load_sem.at[4 + p]) for p in range(pairs)
    ]
    for copy in q_loads:
        copy.start()
    rows = weight.shape[1]
    w_loads = [
        pltpu.make_async_copy(w_hbm.at[pl.ds(pl.multiple_of(head * rows, rows), rows)], weight.at[0], load_sem.at[8]),
        pltpu.make_async_copy(
            w_hbm.at[pl.ds(pl.multiple_of((1 - head) * rows, rows), rows)], weight.at[1], load_sem.at[9]
        ),
    ]

    def at(step):
        return (lax.rem(block + step + cycle, cycle), head)

    place = lax.rem(block, 8)
    relay_one = place < 2
    relay_all = place == 3
    relay = relay_one | relay_all
    forth = jnp.where(relay_one, 8, 7)
    origin = jnp.where(place == 0, 7, jnp.where(place == 1, 5, 4))
    wrapped = relay & (block + forth >= cycle)
    fed_from = jnp.where(place == 2, -7, -8)
    fed = (place <= 2) & (block >= 8)

    def passes(step, piece):
        by_relay = (place == 7) if step == 3 else jnp.bool_(False)
        return by_relay | (place == 7) | ((place == 6) & (step == 3)) if piece >= 2 else by_relay

    def goal(step, piece):
        back = jnp.where((place == 7) & (step == 3), 7, 8)
        return at(jnp.where(passes(step, piece), step - back, step))

    barrier = pltpu.get_barrier_semaphore()

    def signal(semaphore, device):
        pl.semaphore_signal(semaphore, inc=1, device_id=device, device_id_type=MESH)

    for friend in (at(-1), (block, 1 - head), (twin, head)):
        signal(barrier, friend)
    pl.when(place != 2)(lambda: signal(barrier, at(-3)))
    pl.when((place <= 2) & (block < 8))(lambda: signal(barrier, at(fed_from)))

    @pl.when(relay)
    def _():
        signal(barrier, at(origin))
        pl.when(jnp.logical_not(wrapped))(lambda: signal(barrier, at(forth)))

    def enter():
        count = jnp.where(place >= 6, 5, 4) + jnp.where(fed, 1, 0) + jnp.where(wrapped, 1, 0)
        pl.semaphore_wait(barrier, count)
        pl.when(fed)(lambda: signal(ready, at(fed_from)))

    def own_piece(part, piece):
        return own_k.at[part, piece // 2] if piece % 2 else own_v.at[part, piece // 2]

    def met_piece(slot, piece):
        return met_k.at[slot, piece // 2] if piece % 2 else met_v.at[slot, piece // 2]

    def kv_copy(slot, step, piece):
        part = sent_part(step)
        there = jnp.where(passes(step, piece), STEPS - 1, step - 1)
        return pltpu.make_async_remote_copy(
            own_piece(part, piece), met_piece(there, piece), kv_send.at[slot, piece], kv_recv.at[there, piece],
            device_id=goal(step, piece), device_id_type=MESH,
        )

    def sent_part(step):
        return jnp.where(block + step < cycle, 0, 1)

    def keys_start(part):
        both = (sent_part(1) == part) & (sent_part(3) == part)

        @pl.when(both)
        def _():
            for piece in range(1, 2 * groups):
                kv_copy(0, 1, piece).start()
                kv_copy(1, 3, piece).start()

        for step in (1, 3):

            @pl.when((sent_part(step) == part) & jnp.logical_not(both))
            def _():
                for piece in range(1, 2 * groups):
                    kv_copy(step // 2, step, piece).start()

    first_step = jnp.where(even, 1, 3)
    other_step = 4 - first_step

    def hand_copy(piece):
        return pltpu.make_async_remote_copy(
            met_piece(first_step - 1, piece), met_piece(1, piece), kv_send.at[2, piece], kv_recv.at[1, piece],
            device_id=(twin, head), device_id_type=MESH,
        )

    def relay_copy(piece):
        there = jnp.where(place == 0, 0, 2)
        return pltpu.make_async_remote_copy(
            met_piece(STEPS - 1, piece), met_piece(there, piece), kv_send.at[3, piece], kv_recv.at[there, piece],
            device_id=at(forth), device_id_type=MESH,
        )

    def kv_wait(slot, piece):
        pltpu.make_async_remote_copy(
            met_piece(slot, piece), met_piece(slot, piece), kv_send.at[2, piece], kv_recv.at[slot, piece],
            device_id=(twin, head), device_id_type=MESH,
        ).wait_recv()

    for copy in small[3:]:
        copy.wait()
    for part in range(2):
        for group in range(groups):
            own_v[part, group] = v_in[pl.ds(part * half, half), pl.ds(group * HEAD, HEAD)]
    for copy in small[:3]:
        copy.wait()
    lane = lax.broadcasted_iota(jnp.int32, (HEAD, HEAD), 1)
    frequency = freq_in[0:1, :]

    def rotated(block_rows, cut):
        value = block_rows.astype(jnp.float32)
        return (value * cos_tab[cut, :] + pltpu.roll(value, HEAD // 2, 1) * sin_tab[cut, :]).astype(jnp.bfloat16)

    def prepare(part):
        for i in range(half // HEAD):
            cut = pl.ds(pl.multiple_of(part * half + i * HEAD, HEAD), HEAD)
            line = pos_in[pl.ds(part * (half // HEAD) + i, 1), :].astype(jnp.float32)
            column = jnp.transpose(jnp.broadcast_to(line, (HEAD, HEAD)))
            pos_col[cut, :] = column.astype(jnp.int32)
            both = cosine_and_sine(column * frequency, lane)
            other = pltpu.roll(both, HEAD // 2, 1)
            cos_tab[cut, :] = jnp.where(lane < HEAD // 2, both, other)
            sin_tab[cut, :] = jnp.where(lane < HEAD // 2, -other, both)
        cut = pl.ds(pl.multiple_of(part * half, half), half)
        for group in range(groups):
            own_k[part, group] = rotated(k_in[cut, pl.ds(group * HEAD, HEAD)], cut)

    def x_copy(part, order, p):
        cut = pl.ds(pl.multiple_of(part * half, half), half)
        return pltpu.make_async_remote_copy(
            att_own.at[p, cut], att_met.at[p, cut], x_send.at[order, p], x_recv.at[order, p],
            device_id=(block, 1 - head), device_id_type=MESH,
        )

    far = block < STEPS - 1

    first = jnp.where(far, 0, 1)
    second = 1 - first
    alone = jnp.logical_not(far) | (block == 0)

    row_at = lax.broadcasted_iota(jnp.int32, (half, wide), 0)
    key_at = lax.broadcasted_iota(jnp.int32, (half, wide), 1)
    per_group = pairs // groups

    def both_lanes(value):
        return jnp.concatenate([value, value], axis=1)

    def finish(part, p):
        cut = pl.ds(pl.multiple_of(part * half, half), half)
        for n in range(2):
            share = 1.0 / jnp.sum(total[2 * p + n, cut, :], axis=1, keepdims=True)
            att_own[p, cut, n * HEAD : (n + 1) * HEAD] = (sums[2 * p + n, cut, :] * share).astype(jnp.bfloat16)

    def own_block(part, p):
        cut = pl.ds(pl.multiple_of(part * half, half), half)
        group = p // per_group
        keys = own_k[part, group]
        values = own_v[part, group]
        reach = both_lanes(pos_col[cut, :])
        seen = (key_at <= row_at) & (key_at >= row_at - reach)
        for m in range(2):
            lanes = slice(m * HEAD, (m + 1) * HEAD)
            h = 2 * p + m
            query = rotated(q_in[p, cut, lanes], cut)
            q_rot[p, cut, lanes] = query
            scores = lax.dot_general(query, keys, (((1,), (1,)), ((), ())), preferred_element_type=jnp.float32)
            scores = jnp.where(seen, scores, MASKED)
            highest = jnp.broadcast_to(jnp.max(scores, axis=1, keepdims=True), (half, HEAD))
            weights = jnp.exp2((scores - both_lanes(highest)) * scale)
            top[h, cut, :] = highest
            total[h, cut, :] = weights[:, :HEAD] + weights[:, HEAD:]
            sums[h, cut, :] = jnp.dot(weights.astype(jnp.bfloat16), values, preferred_element_type=jnp.float32)

    def pass_on(piece):
        kv_wait(STEPS - 1, piece)
        relay_copy(piece).start()

    def first_own(p, carry):
        own_block(first, p)

        @pl.when(alone)
        def _():
            finish(first, p)
            x_copy(first, 0, p).start()

        @pl.when(p == 0)
        def _():
            prepare(second)
            keys_start(second)

        @pl.when(relay_all & (p == pairs - 2))
        def _():
            pl.when(jnp.logical_not(wrapped))(lambda: pl.semaphore_wait(ready, 1))
            pass_on(0)

        return carry

    def second_own(group, carry):
        for m in range(per_group):
            own_block(second, group * per_group + m)

        @pl.when(relay & (group == 0))
        def _():
            pl.when(relay_all)(lambda: pass_on(1))
            pl.when(relay_one & jnp.logical_not(wrapped))(lambda: pl.semaphore_wait(ready, 1))
            for piece in range(2, 2 * groups):
                pass_on(piece)

        return carry

    prepare(first)
    enter()
    kv_copy(0, 1, 0).start()
    kv_copy(1, 3, 0).start()
    keys_start(first)
    for copy in q_loads:
        copy.wait()
    for copy in w_loads:
        copy.start()
    lax.fori_loop(0, pairs, first_own, 0)
    lax.fori_loop(0, groups, second_own, 0)

    def met_block(step, group):
        early = step <= block
        part = jnp.where(early, 0, 1)
        apart = jnp.where(early, step, cycle - step) * half
        cut = pl.ds(pl.multiple_of(part * half, half), half)
        keys = met_k[step - 1, group]
        values = met_v[step - 1, group]
        reach = both_lanes(pos_col[cut, :])
        seen = key_at >= row_at - reach + apart
        for m in range(2 * per_group):
            p = group * per_group + m // 2
            lanes = slice((m % 2) * HEAD, (m % 2 + 1) * HEAD)
            h = 2 * group * per_group + m
            query = q_rot[p, cut, lanes]
            scores = lax.dot_general(query, keys, (((1,), (1,)), ((), ())), preferred_element_type=jnp.float32)
            scores = jnp.where(seen, scores, MASKED)
            before = top[h, cut, :]
            highest = jnp.maximum(before, jnp.max(scores, axis=1, keepdims=True))
            factor = jnp.exp2((before - highest) * scale)
            weights = jnp.exp2((scores - both_lanes(highest)) * scale)
            top[h, cut, :] = highest
            total[h, cut, :] = total[h, cut, :] * factor + (weights[:, :HEAD] + weights[:, HEAD:])
            sums[h, cut, :] = sums[h, cut, :] * factor + jnp.dot(
                weights.astype(jnp.bfloat16), values, preferred_element_type=jnp.float32
            )
        return part

    def pick(i, usual, one, two):
        def listed(values):
            value = jnp.int32(values[-1])
            for n in range(len(values) - 1):
                value = jnp.where(i == n, values[n], value)
            return value

        return jnp.where(block == 1, listed(one), jnp.where(block == 2, listed(two), listed(usual)))

    def usual_steps(group):
        late = (place < 2) & (group == 1) & (block >= 8)
        return (
            jnp.where(late, other_step, first_step),
            jnp.where(late, first_step, jnp.where(place == 2, 2, other_step)),
            jnp.where(place == 2, other_step, 2),
        )

    def meeting(i, carry):
        group = pick(i, (0, 0, 0, 1, 1, 1), (0, 1, 0, 0, 1, 1), (0, 0, 1, 1, 0, 1))
        turn = pick(i, (-1, -2, -3, -1, -2, -3), (1, 1, 3, 2, 3, 2), (1, 2, 1, 2, 3, 3))
        step = turn
        for n in range(STEPS - 1):
            step = jnp.where(turn == -1 - n, usual_steps(group)[n], step)
        done = pick(i, (0, 0, 1, 0, 0, 1), (1, 1, 0, 1, 0, 1), (0, 1, 0, 1, 1, 1))
        handing = step == first_step

        def arrive(known):
            for piece in (2 * known, 2 * known + 1):
                kv_wait(step - 1, piece)
                pl.when(handing)(lambda: hand_copy(piece).start())

        for known in range(groups):
            pl.when(group == known)(lambda: arrive(known))
        part = met_block(step, group)

        @pl.when(done == 1)
        def _():
            for m in range(per_group):
                p = group * per_group + m
                finish(part, p)
                x_copy(part, jnp.where(part == first, 0, 1), p).start()

        return carry

    lax.fori_loop(0, 2 * (STEPS - 1), meeting, 0)

    tile = 256
    tiles = out_ref.shape[1] // tile

    def project(part, own, met, fresh, last):
        cut = pl.ds(pl.multiple_of(part * half, half), half)

        for t in range(tiles):
            columns = slice(t * tile, (t + 1) * tile)
            value = None if fresh else mixed[cut, columns]
            for which, att, (begin, end) in ((0, att_own, own), (1, att_met, met)):
                if begin < end:
                    left = jnp.concatenate([att[p, cut, :] for p in range(begin, end)], axis=1)
                    right = weight[which, begin * wide : end * wide, columns]
                    more = jnp.dot(left, right, preferred_element_type=jnp.float32)
                    value = more if value is None else value + more
            if last:
                out_ref[cut, columns] = value.astype(jnp.bfloat16)
            else:
                mixed[cut, columns] = value

    for copy in w_loads:
        copy.wait()
    for p in range(pairs):
        x_copy(first, 0, p).wait_recv()
    project(first, (0, pairs), (0, pairs), True, True)
    for p in range(per_group):
        x_copy(second, 1, p).wait_recv()
    project(second, (0, pairs), (0, per_group), True, False)
    for p in range(per_group, pairs):
        x_copy(second, 1, p).wait_recv()
        project(second, (0, 0), (p, p + 1), False, p == pairs - 1)

    for p in range(pairs):
        x_copy(first, 0, p).wait_send()
        x_copy(second, 1, p).wait_send()
    for piece in range(2 * groups):
        kv_copy(0, 1, piece).wait_send()
        kv_copy(1, 3, piece).wait_send()
        hand_copy(piece).wait_send()

    @pl.when(relay)
    def _():
        for piece in range(2, 2 * groups):
            relay_copy(piece).wait_send()

    @pl.when(relay_all)
    def _():
        for piece in range(2):
            relay_copy(piece).wait_send()


def store(value_ref, out_hbm, sem):
    rows = value_ref.shape[0] // sem.shape[0]
    copies = [
        pltpu.make_async_copy(value_ref.at[pl.ds(i * rows, rows)], out_hbm.at[pl.ds(i * rows, rows)], sem.at[i])
        for i in range(sem.shape[0])
    ]
    for copy in copies:
        copy.start()
    for copy in copies:
        copy.wait()


def shards(queries, keys, values, positions, out_weight):
    number, width = queries.shape
    half = number // 2
    pairs = width // (2 * HEAD)
    groups = keys.shape[1] // HEAD
    heads = width // HEAD
    columns = out_weight.shape[1]
    cycle = lax.axis_size("ctx")
    table = np.power(500000.0, -2.0 * np.arange(HEAD // 2) / HEAD).astype(np.float32)
    frequency = jnp.asarray(np.tile(np.concatenate([table, table])[None, :], (8, 1)))
    f32, bf16, i32 = jnp.float32, jnp.bfloat16, jnp.int32
    hbm = pl.BlockSpec(memory_space=pltpu.MemorySpace.HBM)
    projected = pl.pallas_call(
        functools.partial(kernel, cycle),
        name="attend_and_project",
        out_shape=pltpu.VMEM((number, columns), bf16),
        in_specs=[hbm] * 6,
        out_specs=pl.BlockSpec(memory_space=pltpu.MemorySpace.VMEM),
        scratch_shapes=[
            pltpu.VMEM((pairs, number, 2 * HEAD), bf16),
            pltpu.VMEM((number, groups * HEAD), bf16),
            pltpu.VMEM((number, groups * HEAD), bf16),
            pltpu.VMEM((number // HEAD, HEAD), i32),
            pltpu.VMEM((8, HEAD), f32),
            pltpu.VMEM((2, width, columns), bf16),
            pltpu.VMEM((number, HEAD), i32),
            pltpu.VMEM((number, HEAD), f32),
            pltpu.VMEM((number, HEAD), f32),
            pltpu.VMEM((pairs, number, 2 * HEAD), bf16),
            pltpu.VMEM((2, groups, half, HEAD), bf16),
            pltpu.VMEM((2, groups, half, HEAD), bf16),
            pltpu.VMEM((STEPS, groups, half, HEAD), bf16),
            pltpu.VMEM((STEPS, groups, half, HEAD), bf16),
            pltpu.VMEM((heads, number, HEAD), f32),
            pltpu.VMEM((heads, number, HEAD), f32),
            pltpu.VMEM((heads, number, HEAD), f32),
            pltpu.VMEM((pairs, number, 2 * HEAD), bf16),
            pltpu.VMEM((pairs, number, 2 * HEAD), bf16),
            pltpu.VMEM((number, columns), f32),
            pltpu.SemaphoreType.DMA((10,)),
            pltpu.SemaphoreType.DMA((STEPS, 2 * groups)),
            pltpu.SemaphoreType.DMA((STEPS, 2 * groups)),
            pltpu.SemaphoreType.DMA((2, pairs)),
            pltpu.SemaphoreType.DMA((2, pairs)),
            pltpu.SemaphoreType.REGULAR,
        ],
        compiler_params=pltpu.CompilerParams(collective_id=0, has_side_effects=True, vmem_limit_bytes=60 << 20),
    )(queries, keys, values, positions.reshape(number // HEAD, HEAD), frequency, out_weight)
    return pl.pallas_call(
        store,
        name="store",
        out_shape=jax.ShapeDtypeStruct((number, columns), bf16),
        in_specs=[pl.BlockSpec(memory_space=pltpu.MemorySpace.VMEM)],
        out_specs=pl.BlockSpec(memory_space=pltpu.MemorySpace.HBM),
        scratch_shapes=[pltpu.SemaphoreType.DMA((4,))],
    )(pltpu.with_memory_space_constraint(projected, pltpu.MemorySpace.VMEM))


def solution(mesh):
    in_specs = (P("ctx", "head"), P("ctx", "head"), P("ctx", "head"), P("ctx"), P(None, "head"))
    out_specs = P("ctx", "head")
    return jax.shard_map(shards, mesh=mesh, in_specs=in_specs, out_specs=out_specs, check_vma=False)
```
